256 devices in a mesh: ka: 8 (over y_lo, x), hist: 32 (over y_hi, z, core).
Axes of the slice: x: 4, y: 4 (y_hi: 2, y_lo: 2; y = y_hi * 2 + y_lo), z: 8, core: 2. Of those that a mesh axis runs over, the one named last changes fastest.
Arguments:
- step_index: int32 [1], replicated, may hold values from 33 to 128
- band_energy: float32 [128, 3, 1024], P('hist', None, 'ka'), may hold values from -1 to 3
- kernel_row: bfloat16 [128, 2, 3, 3, 1024], P('hist', None, None, None, 'ka'), may hold values from -0.5 to 0.5
- lattice_history: bfloat16 [128, 2, 3, 3, 128, 1024], P('hist', None, None, None, None, 'ka'), may hold values from -6 to 6, as said below
- diagonal_inverse: float32 [2, 3, 3, 1024], P(None, None, None, 'ka'), may hold values from -3 to 3
- multiplicity: int32 [1024], P('ka'), may hold values from 1 to 32, as said below
- state_energy: float32 [64], replicated, may hold values from -3 to 3
- connection: int32 [64, 6], replicated, may hold values from 0 to 63, as said below
- predicted_row: float32 [2, 64, 128], P(None, None, 'hist'), may hold values from -6 to 6
- pseudo_history: bfloat16 [128, 2, 64, 128], P('hist'), may hold values from -6 to 6, as said below
Outputs:
- lattice_row: bfloat16 [128, 2, 3, 3, 1024], P('hist', None, None, None, 'ka')
- local_row: float32 [2, 3, 3, 128], P(None, None, None, 'hist')
- pseudo_row: float32 [2, 64, 128], P(None, None, 'hist')
The draws below stay inside these ranges and needn't reach their ends.
Inputs may be any that keep to these rules, and one draw needn't show every extreme that they name: `lattice_history`: the stored lattice propagators vanish where the column time j exceeds the row time m. `pseudo_history`: the stored pseudo-particle propagators vanish where the column time j exceeds the row time m. `multiplicity`: powers of two. For each flavour f, s -> connection[s, f] is an involution without fixed points; two states that flavour f links differ in that flavour's occupation, under a numbering of the states drawn from the seed.
All inputs are finite; a program needn't handle non-finite values.
Results may differ from the reference program's by a relative error of at most 0.012.
Values may be sent and summed in bfloat16 or wider, within the bound.
No kernel may reach another device: no remote copies, remote signals or barrier semaphores. Data moves between devices by JAX's collectives and lax.ppermute only.
A program may use at most 64 MiB of HBM per device.

```python
import math
import jax
import jax.numpy as jnp
from jax import lax

ORB = 3
FLAV = 6
STATES = 64
K_DEV = 128
TIMES = 128
KPTS = 1024
N_KA = 8


def draw_kernel_row(key, part):
    first, second = jax.random.split(jax.random.fold_in(key, 11), 2)
    spread = 0.6 / math.sqrt(3.0 * TIMES)
    common = jax.random.normal(first, (TIMES, 2, 3, 3, 1), jnp.float32)
    own = jax.random.normal(second, (TIMES, 2, 3, 3, KPTS), jnp.float32)
    values = (common + own) * spread
    return jnp.clip(values, -0.5, 0.5).astype(jnp.bfloat16)


def causal_mask(length):
    rows = jnp.arange(length, dtype=jnp.int32)
    return (rows[None, :] <= rows[:, None]).astype(jnp.float32)


def draw_lattice_history(key, part):
    first, second = jax.random.split(jax.random.fold_in(key, 23), 2)
    common = jax.random.normal(first, (TIMES, 2, 3, 3, TIMES, 1), jnp.float32)
    own = jax.random.normal(second, (TIMES, 2, 3, 3, TIMES, KPTS), jnp.float32)
    values = 0.7 * common + 0.7 * own
    mask = causal_mask(TIMES)[:, None, None, None, :, None]
    return (jnp.clip(values, -6.0, 6.0) * mask).astype(jnp.bfloat16)


def draw_pseudo_history(key, part):
    first = jax.random.fold_in(jax.random.fold_in(key, 37), 0)
    values = jax.random.normal(first, (TIMES, 2, STATES, TIMES), jnp.float32)
    mask = causal_mask(TIMES)[:, None, None, :]
    return (jnp.clip(values, -6.0, 6.0) * mask).astype(jnp.bfloat16)


def draw_diagonal_inverse(key, part):
    first, second, third = jax.random.split(jax.random.fold_in(key, 41), 3)
    identity = jnp.eye(3, dtype=jnp.float32)[:, :, None]
    diag_part = 0.2 * jax.random.normal(first, (3, 3, KPTS), jnp.float32)
    off_real = 0.3 * jax.random.normal(second, (3, 3, KPTS), jnp.float32)
    off_imag = 0.3 * jax.random.normal(third, (3, 3, KPTS), jnp.float32)
    part_real = identity * (1.0 + diag_part) + (1.0 - identity) * off_real
    return jnp.clip(jnp.stack([part_real, off_imag], axis=0), -3.0, 3.0)


def draw_multiplicity(key, part):
    index = jnp.arange(KPTS, dtype=jnp.int32)
    highest = 2 + 4 * index // KPTS
    powers = jax.random.randint(jax.random.fold_in(key, 53), (KPTS,), 0, highest + 1)
    return jnp.left_shift(jnp.ones((KPTS,), jnp.int32), powers)


def draw_connection(key, part):
    labels = jax.random.permutation(jax.random.fold_in(key, 67), STATES)
    positions = jnp.argsort(labels, stable=True).astype(jnp.int32)
    flips = jnp.left_shift(jnp.ones((FLAV,), jnp.int32), jnp.arange(FLAV, dtype=jnp.int32))
    target = jnp.bitwise_xor(positions[:, None], flips[None, :])
    return labels[target].astype(jnp.int32)


def block_levels(stream_key, dims, cuts, low, top_value):
    def one(axis_at, blocks):
        heights = jax.random.uniform(jax.random.fold_in(jax.random.fold_in(stream_key, 6), axis_at), (blocks,), jnp.float32, low / len(cuts), top_value / len(cuts))
        return jnp.repeat(jnp.exp(heights), dims[axis_at] // blocks).reshape((-1,) + (1,) * (len(dims) - axis_at - 1))

    factor_of = one(*cuts[0])
    for cut in cuts[1:]:
        factor_of = factor_of * one(*cut)
    return factor_of


def centred(key, extent, deviation, most, shards=(), held_as=jnp.bfloat16):
    array = deviation * jax.random.normal(key, extent, jnp.float32)
    if shards:
        array = array * block_levels(key, extent, shards, -0.22, 0.18)
    return jnp.clip(array, -most, most).astype(held_as)


def setup_inputs(seed: int = 0) -> dict:
    splits = jax.random.split(jax.random.key(seed), 11)
    step_index = jax.random.randint(splits[0], (1,), TIMES // 4 + 1, TIMES + 1).astype(jnp.int32)
    band_energy = jnp.clip(-1.0 + 4.0 * jax.random.uniform(splits[1], (TIMES, ORB, KPTS), jnp.float32) ** block_levels(splits[1], (TIMES, ORB, KPTS), ((0, 32), (2, 8)), -0.2, 0.2), -1.0, 3.0)
    kernel_row = draw_kernel_row(jax.random.fold_in(splits[10], 71), 0)
    lattice_history = draw_lattice_history(jax.random.fold_in(splits[10], 71), 0)
    diagonal_inverse = draw_diagonal_inverse(jax.random.fold_in(splits[10], 71), 0)
    multiplicity = draw_multiplicity(jax.random.fold_in(splits[10], 71), 0)
    state_energy = jnp.clip(jax.random.uniform(splits[6], (STATES,), jnp.float32, -3.0, 3.0), -3.0, 3.0)
    connection = draw_connection(jax.random.fold_in(splits[10], 71), 0)
    predicted_row = centred(splits[8], (2, STATES, TIMES), 1.0, 6.0, ((2, 32),), jnp.float32)
    pseudo_history = draw_pseudo_history(jax.random.fold_in(splits[10], 71), 0)
    return dict(step_index=step_index, band_energy=band_energy, kernel_row=kernel_row, lattice_history=lattice_history, diagonal_inverse=diagonal_inverse, multiplicity=multiplicity, state_energy=state_energy, connection=connection, predicted_row=predicted_row, pseudo_history=pseudo_history)


time_step = 0.05
coupling = 0.02


def complex_form(kernel):
    part_real = kernel[:, 0]
    part_imag = kernel[:, 1]
    upper = jnp.stack([part_real, -part_imag], axis=2)
    lower_half = jnp.stack([part_imag, part_real], axis=2)
    return jnp.stack([upper, lower_half], axis=1)


def contract(matrix, vector):
    return jnp.einsum('abk,jbck->jack', matrix, vector, precision=lax.Precision.HIGHEST)


def reference(step_index, band_energy, kernel_row, lattice_history, diagonal_inverse, multiplicity, state_energy, connection, predicted_row, pseudo_history):
    current = step_index[0]
    all_times = jnp.arange(TIMES, dtype=jnp.int32)
    before_now = (all_times < current).astype(jnp.float32)
    weight = jnp.where(all_times == 0, 0.5, 1.0).astype(jnp.float32) * before_now
    in_range = (all_times <= current).astype(jnp.float32)
    earlier = jnp.cumsum(band_energy, axis=0) - band_energy
    upto_now = jnp.sum(band_energy * before_now[:, None, None], axis=0)
    angles = time_step * (upto_now[None] - earlier)
    free_pair = jnp.stack([-jnp.sin(angles), -jnp.cos(angles)], axis=1) * in_range[:, None, None, None]
    identity = jnp.eye(3, dtype=jnp.float32)
    free_rows = free_pair[:, :, :, None, :] * identity[None, None, :, :, None]
    kernel = kernel_row.astype(jnp.float32) * weight[:, None, None, None, None]
    kernel_pairs = complex_form(kernel)
    pieces = []
    for k_block in range(N_KA):
        lower_k = k_block * K_DEV
        upper_k = lower_k + K_DEV
        pieces.append(jnp.einsum('msapbk,mpbcjk->jsack', kernel_pairs[..., lower_k:upper_k], lattice_history[..., lower_k:upper_k].astype(jnp.float32), precision=lax.Precision.HIGHEST))
    volterra_terms = jnp.concatenate(pieces, axis=4)
    right_side = volterra_terms + free_rows
    out_real = contract(diagonal_inverse[0], right_side[:, 0]) - contract(diagonal_inverse[1], right_side[:, 1])
    out_imag = contract(diagonal_inverse[0], right_side[:, 1]) + contract(diagonal_inverse[1], right_side[:, 0])
    fresh_rows = jnp.stack([out_real, out_imag], axis=1)
    lattice_row = fresh_rows.astype(jnp.bfloat16)
    weights_k = multiplicity.astype(jnp.float32)
    summed = jnp.einsum('jsack,k->sacj', fresh_rows, weights_k, precision=lax.Precision.HIGHEST)
    local_rows = summed / jnp.sum(weights_k)
    hybrid = jnp.repeat(jnp.diagonal(local_rows, axis1=1, axis2=2), 2, axis=2)
    hyb_real = hybrid[0].T
    hyb_imag = hybrid[1].T
    onehot = (connection[:, :, None] == jnp.arange(STATES, dtype=jnp.int32)[None, None, :]).astype(jnp.float32)
    reached = jnp.einsum('sft,ptm->psfm', onehot, predicted_row, precision=lax.Precision.HIGHEST)
    self_real = coupling * jnp.sum(hyb_real[None] * reached[0] - hyb_imag[None] * reached[1], axis=1)
    self_imag = coupling * jnp.sum(hyb_real[None] * reached[1] + hyb_imag[None] * reached[0], axis=1)
    wself_real = (self_real * weight[None, :]).T
    wself_imag = (self_imag * weight[None, :]).T
    hist_real = pseudo_history[:, 0].astype(jnp.float32)
    hist_imag = pseudo_history[:, 1].astype(jnp.float32)
    sum_real = jnp.sum(wself_real[:, :, None] * hist_real - wself_imag[:, :, None] * hist_imag, axis=0)
    sum_imag = jnp.sum(wself_real[:, :, None] * hist_imag + wself_imag[:, :, None] * hist_real, axis=0)
    elapsed = (current - all_times).astype(jnp.float32)
    spins = state_energy[:, None] * time_step * elapsed[None, :]
    pseudo_real = -jnp.sin(spins) * in_range[None, :] + sum_real
    pseudo_imag = -jnp.cos(spins) * in_range[None, :] + sum_imag
    pseudo_row = jnp.stack([pseudo_real, pseudo_imag], axis=0)
    return lattice_row, local_rows, pseudo_row
```

```python
import jax
import jax.numpy as jnp
from jax import lax
from jax.experimental import pallas as pl
from jax.experimental.pallas import tpu as pltpu
from jax.sharding import PartitionSpec as P

time_step = 0.05
coupling = 0.02
F32 = jnp.float32
BF16 = jnp.bfloat16
ROWS = 80
CHUNKS = 4
HIGHEST = lax.Precision.HIGHEST


def split_high_low(x):
    high = x.astype(BF16).astype(F32)
    return high, x - high


def energy_rows(total):
    high, low = split_high_low(total)
    return jnp.concatenate([high, low, jnp.zeros((2, total.shape[1]), F32)], axis=0)


def terms_kernel(meta, kernel_row, energy, history, own, other, coeff, store, sems):
    current, position = meta[0], meta[1]
    wide = history.shape[4] // CHUNKS

    def fetch(i):
        columns = pl.ds(pl.multiple_of(i * wide, wide), wide)
        return pltpu.make_async_copy(
            history.at[:, :, :, :, columns, :], store.at[:, :, :, :, columns, :], sems.at[i]
        )

    for i in range(CHUNKS):
        fetch(i).start()
    block = kernel_row.shape[0]
    total = jnp.zeros(energy.shape[1:], F32)
    for m in range(block):
        time = position * block + m
        weight = jnp.where(time < current, jnp.where(time == 0, 0.5, 1.0), 0.0).astype(F32)
        total = total + energy[m] * jnp.where(time < current, 1.0, 0.0).astype(F32)
        for s in range(2):
            for a in range(3):
                rows = kernel_row[m, s, a].astype(F32) * weight
                for b in range(3):
                    coeff[m, s, a, b] = jnp.broadcast_to(rows[b : b + 1], (8, rows.shape[1]))
    rows_sent = energy_rows(total)
    low_half = lax.broadcasted_iota(jnp.int32, (8, 128), 0) < 4
    even_core = position % 2 == 0

    def sixteen(start, pair):
        groups = [[], []]
        for c in range(3):
            acc = {}
            for m in range(block):
                for b in range(3):
                    columns = pl.ds(pl.multiple_of(start, 16), 16)
                    re = store[m, 0, b, c, columns, :].astype(F32)
                    im = store[m, 1, b, c, columns, :].astype(F32)
                    for a in range(3):
                        kr = coeff[m, 0, a, b]
                        ki = coeff[m, 1, a, b]
                        for g in range(2):
                            hr, hi = re[8 * g : 8 * g + 8], im[8 * g : 8 * g + 8]
                            x = kr * hr - ki * hi
                            y = kr * hi + ki * hr
                            acc[0, a, g] = x if m + b == 0 else acc[0, a, g] + x
                            acc[1, a, g] = y if m + b == 0 else acc[1, a, g] + y
            for g in range(2):
                groups[g] += [acc[s, a, g] for s in range(2) for a in range(3)]
        for g in range(2):
            chip = pair + g
            evens, odds = [], []
            for u in range(9):
                p, q = groups[g][2 * u], groups[g][2 * u + 1]
                evens.append(jnp.where(low_half, p, pltpu.roll(q, 4, 0)))
                odds.append(jnp.where(low_half, pltpu.roll(p, 4, 0), q))
            evens.append(rows_sent * jnp.where(position > 2 * chip, 1.0, 0.0).astype(F32))
            odds.append(rows_sent * jnp.where(position > 2 * chip + 1, 1.0, 0.0).astype(F32))
            even = jnp.concatenate(evens, axis=0).astype(BF16)
            odd = jnp.concatenate(odds, axis=0).astype(BF16)
            own[chip] = jnp.where(even_core, even, odd)
            other[chip] = jnp.where(even_core, odd, even)

    @pl.loop(0, CHUNKS)
    def _(i):
        fetch(i).wait()

        @pl.loop(0, wide // 16)
        def _(h):
            sixteen(i * wide + h * 16, i * (wide // 8) + 2 * h)


def add_kernel(own, arrived, out):
    @pl.loop(0, own.shape[0])
    def _(i):
        x = own[i].astype(F32) + arrived[i].astype(F32)
        energies = energy_rows(x[72:75] + x[75:78])
        out[i] = jnp.concatenate([x[:72], energies], axis=0).astype(BF16)


def rows_kernel(meta, arrived, energy, inverse, multiplicity, fresh, sums):
    current, position = meta[0], meta[1]
    block = energy.shape[0]
    got = arrived[0].astype(F32)
    for i in range(1, arrived.shape[0]):
        got = got + arrived[i].astype(F32)
    later = got[72:75] + got[75:78]
    ends = []
    for m in reversed(range(block)):
        later = later + energy[m] * jnp.where(position * block + m < current, 1.0, 0.0).astype(F32)
        ends.append(later)
    angle = jnp.concatenate(
        [jnp.concatenate([ends[block - 1 - j][a : a + 1] for j in range(block)], axis=0) for a in range(3)],
        axis=0,
    ) * time_step
    column = lax.broadcasted_iota(jnp.int32, angle.shape, 0) % block + position * block
    in_range = (column <= current).astype(F32)
    free = [-jnp.sin(angle) * in_range, -jnp.cos(angle) * in_range]

    def right(s, b, c):
        r = ((c * 2 + s) * 3 + b) * block
        x = got[r : r + block]
        return x + free[s][b * block : (b + 1) * block] if b == c else x

    result = {}
    for c in range(3):
        side = {(s, b): right(s, b, c) for s in range(2) for b in range(3)}
        for a in range(3):
            re = im = 0.0
            for b in range(3):
                dr, di = inverse[0, a, b : b + 1, :], inverse[1, a, b : b + 1, :]
                re = re + dr * side[0, b] - di * side[1, b]
                im = im + dr * side[1, b] + di * side[0, b]
            result[0, a, c], result[1, a, c] = re, im
    entries = [result[s, a, c] for s in range(2) for a in range(3) for c in range(3)]
    for i, x in enumerate(entries):
        fresh[i] = x
    lanes = got.shape[1]
    entries += [jnp.ones((1, lanes), F32), jnp.zeros((lanes - 73, lanes), F32)]
    table = jnp.concatenate(entries, axis=0)
    weights = jnp.broadcast_to(multiplicity[...].astype(F32), (8, lanes))
    sums[...] = lax.dot_general(
        weights, table, (((1,), (1,)), ((), ())), precision=HIGHEST, preferred_element_type=F32
    )


VMEM = pl.BlockSpec(memory_space=pltpu.VMEM)
SMEM = pl.BlockSpec(memory_space=pltpu.SMEM)
ANY = pl.BlockSpec(memory_space=pl.ANY)


def per_device(
    step_index,
    band_energy,
    kernel_row,
    lattice_history,
    diagonal_inverse,
    multiplicity,
    state_energy,
    connection,
    predicted_row,
    pseudo_history,
):
    current = step_index[0]
    block = band_energy.shape[0]
    lanes = band_energy.shape[2]
    hist_size = lax.axis_size("hist")
    chips = hist_size // 2
    position = lax.axis_index("hist")
    meta = jnp.stack([current, position.astype(jnp.int32)])
    owned_times = position * block + jnp.arange(block, dtype=jnp.int32)
    before_now = (owned_times < current).astype(F32)
    weight = jnp.where(owned_times == 0, 0.5, 1.0).astype(F32) * before_now
    in_range = (owned_times <= current).astype(F32)
    tiles = jax.ShapeDtypeStruct((chips, ROWS, lanes), BF16)

    own, other = pl.pallas_call(
        terms_kernel,
        out_shape=(tiles, tiles),
        in_specs=[SMEM, VMEM, VMEM, ANY],
        out_specs=(VMEM, VMEM),
        scratch_shapes=[
            pltpu.VMEM((block, 2, 3, 3, 8, lanes), F32),
            pltpu.VMEM(lattice_history.shape, BF16),
            pltpu.SemaphoreType.DMA((CHUNKS,)),
        ],
        compiler_params=pltpu.CompilerParams(vmem_limit_bytes=32 << 20),
        name="terms",
    )(meta, kernel_row, band_energy, lattice_history)
    swapped = lax.ppermute(other, "hist", [(h, h ^ 1) for h in range(hist_size)])
    paired = pl.pallas_call(
        add_kernel,
        out_shape=tiles,
        in_specs=[VMEM, VMEM],
        out_specs=VMEM,
        name="add_pair",
    )(own, swapped)
    same_core = [[2 * t + c for t in range(chips)] for c in range(2)]
    arrived = lax.all_to_all(
        paired, "hist", split_axis=0, concat_axis=0, tiled=True, axis_index_groups=same_core
    )
    fresh, sums = pl.pallas_call(
        rows_kernel,
        out_shape=(
            jax.ShapeDtypeStruct((18, block, lanes), F32),
            jax.ShapeDtypeStruct((8, lanes), F32),
        ),
        in_specs=[SMEM, VMEM, VMEM, VMEM, VMEM],
        out_specs=(VMEM, VMEM),
        name="rows",
    )(meta, arrived, band_energy, diagonal_inverse, multiplicity.reshape(1, lanes))
    lattice_row = (
        jnp.transpose(fresh, (1, 0, 2)).reshape(block, 2, 3, 3, lanes).astype(BF16)
    )
    shared = lax.all_to_all(
        sums[:, None, :], "ka", split_axis=0, concat_axis=0, tiled=True
    )
    summed = jnp.sum(shared, axis=(0, 1))
    local_rows = (summed[:72] / summed[72]).reshape(2, 3, 3, block)

    diag = jnp.stack([local_rows[:, a, a, :] for a in range(3)], axis=1)
    states = connection.shape[0]
    onehot = (
        connection[:, :, None] == jnp.arange(states, dtype=jnp.int32)[None, None, :]
    ).astype(F32)
    by_orbital = onehot.reshape(states, 3, 2, states).sum(axis=2)
    reached = jnp.einsum("sat,ptm->psam", by_orbital, predicted_row, precision=HIGHEST)
    self_real = coupling * jnp.sum(diag[0][None] * reached[0] - diag[1][None] * reached[1], axis=1)
    self_imag = coupling * jnp.sum(diag[0][None] * reached[1] + diag[1][None] * reached[0], axis=1)
    wself_real = (self_real * weight[None, :]).T
    wself_imag = (self_imag * weight[None, :]).T
    hist_real = pseudo_history[:, 0].astype(F32)
    hist_imag = pseudo_history[:, 1].astype(F32)
    sum_real = jnp.sum(
        wself_real[:, :, None] * hist_real - wself_imag[:, :, None] * hist_imag, axis=0
    )
    sum_imag = jnp.sum(
        wself_real[:, :, None] * hist_imag + wself_imag[:, :, None] * hist_real, axis=0
    )
    part = jnp.stack([sum_real, sum_imag], axis=0).astype(BF16)
    part = part.reshape(2, states, hist_size, block).transpose(2, 0, 1, 3)
    shares = lax.all_to_all(part, "hist", split_axis=0, concat_axis=0, tiled=True)
    shares = shares.astype(F32).sum(axis=0)
    elapsed = (current - owned_times).astype(F32)
    spins = state_energy[:, None] * time_step * elapsed[None, :]
    free_pseudo = jnp.stack([-jnp.sin(spins), -jnp.cos(spins)], axis=0) * in_range[None, None, :]
    return (lattice_row, local_rows, free_pseudo + shares)


def solution(mesh):
    in_specs = (
        P(),
        P("hist", None, "ka"),
        P("hist", None, None, None, "ka"),
        P("hist", None, None, None, None, "ka"),
        P(None, None, None, "ka"),
        P("ka"),
        P(),
        P(),
        P(None, None, "hist"),
        P("hist", None, None, None),
    )
    out_specs = (
        P("hist", None, None, None, "ka"),
        P(None, None, None, "hist"),
        P(None, None, "hist"),
    )
    return jax.shard_map(
        per_device, mesh=mesh, in_specs=in_specs, out_specs=out_specs, check_vma=False
    )
```

```python
import jax
import jax.numpy as jnp
from jax import lax
from jax.experimental import pallas as pl
from jax.experimental.pallas import tpu as pltpu
from jax.sharding import PartitionSpec as P

time_step = 0.05
coupling = 0.02
F32 = jnp.float32
BF16 = jnp.bfloat16
HIGHEST = lax.Precision.HIGHEST
TERMS = 80
INPUTS = 24
CHUNKS = 4


def flag(condition):
    return jnp.where(condition, 1.0, 0.0).astype(F32)


def low_half(lanes=128):
    return lax.broadcasted_iota(jnp.int32, (8, lanes), 0) < 4


def high_low(x):
    high = x.astype(BF16).astype(F32)
    return jnp.where(low_half(x.shape[1]), high, x - high)


def interleave(p, q):
    low = low_half(p.shape[1])
    return jnp.where(low, p, pltpu.roll(q, 4, 0)), jnp.where(low, pltpu.roll(p, 4, 0), q)


def terms_kernel(step, kernel_row, energy, predicted, pseudo, history, own, other, coeff, turned, store, sems):
    current, position = step[0], lax.axis_index("hist")
    wide = history.shape[4] // CHUNKS

    def fetch(i):
        columns = pl.ds(pl.multiple_of(i * wide, wide), wide)
        return pltpu.make_async_copy(
            history.at[:, :, :, :, columns, :], store.at[:, :, :, :, columns, :], sems.at[i]
        )

    for i in range(CHUNKS):
        fetch(i).start()
    block = energy.shape[1]
    lanes = energy.shape[2]
    zero = jnp.zeros((1, lanes), F32)
    total = jnp.zeros((3, lanes), F32)
    for m in range(block):
        time = position * block + m
        weight = jnp.where(time < current, jnp.where(time == 0, 0.5, 1.0), 0.0).astype(F32)
        total = total + energy[:, m, :] * flag(time < current)
        for a in range(3):
            for b in range(3):
                rows = kernel_row[m, a, b].astype(F32) * weight
                for s in range(2):
                    coeff[m, s, a, b] = jnp.broadcast_to(rows[s : s + 1], (8, lanes))
        both = jnp.concatenate([pseudo[m, 0], pseudo[m, 1]], axis=0).astype(F32)
        turned[m] = both.T
    energies = high_low(jnp.concatenate([total, zero, total, zero], axis=0))
    ahead = jnp.concatenate([predicted[0], predicted[1]], axis=1)
    ahead = high_low(jnp.concatenate([ahead, ahead], axis=0))
    even_core = position % 2 == 0

    def sixteen(start, pair):
        groups = [[], []]
        for c in range(3):
            acc = {}
            for m in range(block):
                for b in range(3):
                    columns = pl.ds(pl.multiple_of(start, 16), 16)
                    re = store[m, 0, b, c, columns, :].astype(F32)
                    im = store[m, 1, b, c, columns, :].astype(F32)
                    for a in range(3):
                        kr = coeff[m, 0, a, b]
                        ki = coeff[m, 1, a, b]
                        for g in range(2):
                            hr, hi = re[8 * g : 8 * g + 8], im[8 * g : 8 * g + 8]
                            x = kr * hr - ki * hi
                            y = kr * hi + ki * hr
                            acc[0, a, g] = x if m + b == 0 else acc[0, a, g] + x
                            acc[1, a, g] = y if m + b == 0 else acc[1, a, g] + y
            for g in range(2):
                groups[g] += [acc[s, a, g] for s in range(2) for a in range(3)]
        for g in range(2):
            chip = pair + g
            evens, odds = [], []

            def add(p, q):
                x, y = interleave(p, q)
                evens.append(x)
                odds.append(y)

            for u in range(9):
                add(groups[g][2 * u], groups[g][2 * u + 1])
            evens.append(energies * flag(position > 2 * chip))
            odds.append(energies * flag(position > 2 * chip + 1))
            columns = pl.ds(pl.multiple_of(start + 8 * g, 8), 8)
            for m in range(0, block, 2):
                add(turned[m, columns, :], turned[m + 1, columns, :])
            evens.append(ahead)
            odds.append(ahead)
            even = jnp.concatenate(evens, axis=0).astype(BF16)
            odd = jnp.concatenate(odds, axis=0).astype(BF16)
            own[chip] = jnp.where(even_core, even, odd)
            other[chip] = jnp.where(even_core, odd, even)

    @pl.loop(0, CHUNKS)
    def _(i):
        fetch(i).wait()

        @pl.loop(0, wide // 16)
        def _(h):
            sixteen(i * wide + h * 16, i * (wide // 8) + 2 * h)


def add_kernel(own, arrived, out):
    @pl.loop(0, own.shape[0] // 4)
    def _(i):
        for u in range(4):
            t = 4 * i + u
            x = own[t, :TERMS].astype(F32) + arrived[t, :TERMS].astype(F32)
            energies = x[72:80]
            energies = high_low(energies + pltpu.roll(energies, 4, 0))
            out[t, :TERMS] = jnp.concatenate([x[:72], energies], axis=0).astype(BF16)
            out[t, TERMS : TERMS + INPUTS] = own[t, TERMS:]
            out[t, TERMS + INPUTS :] = arrived[t, TERMS:]


def rows_kernel(step, arrived, energy, inverse, multiplicity, fresh, sums):
    current, position = step[0], lax.axis_index("hist")
    block = energy.shape[1]
    lanes = energy.shape[2]
    got = arrived[0, :TERMS].astype(F32)
    for i in range(1, arrived.shape[0]):
        got = got + arrived[i, :TERMS].astype(F32)
    later = got[72:75] + got[76:79]
    ends = []
    for m in reversed(range(block)):
        later = later + energy[:, m, :] * flag(position * block + m < current)
        ends.append(later)
    angle = jnp.concatenate(
        [ends[block - 1 - j][a : a + 1] for a in range(3) for j in range(block)], axis=0
    )
    angle = angle * time_step
    column = lax.broadcasted_iota(jnp.int32, angle.shape, 0) % block + position * block
    in_range = (column <= current).astype(F32)
    free = [-jnp.sin(angle) * in_range, -jnp.cos(angle) * in_range]

    def right(s, b, c):
        r = ((c * 2 + s) * 3 + b) * block
        x = got[r : r + block]
        return x + free[s][b * block : (b + 1) * block] if b == c else x

    entries = {}
    for c in range(3):
        side = {(s, b): right(s, b, c) for s in range(2) for b in range(3)}
        for a in range(3):
            re = im = 0.0
            for b in range(3):
                dr, di = inverse[a, b, 0:1, :], inverse[a, b, 1:2, :]
                re = re + dr * side[0, b] - di * side[1, b]
                im = im + dr * side[1, b] + di * side[0, b]
            entries[a, c, 0], entries[a, c, 1] = re, im
    entries = [entries[a, c, s] for a in range(3) for c in range(3) for s in range(2)]
    for i, x in enumerate(entries):
        fresh[i] = x
    entries += [jnp.ones((1, lanes), F32), jnp.zeros((lanes - 73, lanes), F32)]
    table = jnp.concatenate(entries, axis=0)
    weights = jnp.broadcast_to(multiplicity[...].astype(F32), (8, lanes))
    message = lax.dot_general(
        weights, table, (((1,), (1,)), ((), ())), precision=HIGHEST, preferred_element_type=F32
    )
    for i in range(0, sums.shape[0], 8):
        sums[i : i + 8] = message


def signed_swap(x):
    lanes = x.shape[1]
    swapped = pltpu.roll(x, lanes // 2, 1)
    lower = lax.broadcasted_iota(jnp.int32, x.shape, 1) < lanes // 2
    return jnp.where(lower, -swapped, swapped)


def prepare_kernel(step, arrived, links, levels, fresh, product, free, lattice, high, low, raw, reached):
    current, position = step[0], lax.axis_index("hist")
    chips = arrived.shape[0]
    states = links.shape[1]
    block = fresh.shape[1]
    even_core = position % 2 == 0

    @pl.loop(0, chips)
    def _(t):
        mine = arrived[t, TERMS : TERMS + INPUTS].astype(F32)
        near = arrived[t, TERMS + INPUTS :].astype(F32)
        even = jnp.where(even_core, mine, near)
        odd = jnp.where(even_core, near, mine)
        raw[2 * t] = even[:16]
        raw[2 * t + 1] = odd[:16]
        times = pl.ds(pl.multiple_of(8 * t, 8), 8)
        high[times, :], low[times, :] = interleave(even[16:], odd[16:])

    state = lax.broadcasted_iota(jnp.int32, (states, states), 0)
    for a in range(3):
        link = flag(links[2 * a : 2 * a + 1, :] == state) + flag(links[2 * a + 1 : 2 * a + 2, :] == state)
        link = jnp.concatenate([link, link], axis=1).astype(BF16)
        for p in range(2):
            half = slice(p * states, (p + 1) * states)
            part = jnp.dot(high[:, half].astype(BF16), link, preferred_element_type=F32)
            part = part + jnp.dot(low[:, half].astype(BF16), link, preferred_element_type=F32)
            reached[a, p] = part

    @pl.loop(0, chips)
    def _(t):
        times = pl.ds(pl.multiple_of(8 * t, 8), 8)
        time = lax.broadcasted_iota(jnp.int32, (8, 2 * states), 0) + 8 * t
        weight = jnp.where(time < current, jnp.where(time == 0, 0.5, 1.0), 0.0) * coupling
        for j in range(block):
            first = raw[2 * t, pl.ds(j, 4, stride=4), :]
            second = raw[2 * t + 1, pl.ds(j, 4, stride=4), :]
            past = jnp.concatenate([first, second], axis=0) * weight.astype(F32)
            for a in range(3):
                x = reached[a, 0, times, :] * past
                y = reached[a, 1, times, :] * past
                product[a, j, times, :] = x + signed_swap(y)

    column = lax.broadcasted_iota(jnp.int32, (block, 2 * states), 0) + position * block
    elapsed = (current - column).astype(F32)
    level = jnp.concatenate([levels[...], levels[...]], axis=1)
    spin = level * time_step * elapsed
    lower = lax.broadcasted_iota(jnp.int32, spin.shape, 1) < states
    free[...] = jnp.where(lower, -jnp.sin(spin), -jnp.cos(spin)) * (column <= current).astype(F32)
    for a in range(3):
        for c in range(3):
            i = (a * 3 + c) * 2
            re, im = fresh[i], fresh[i + 1]
            for j in range(block):
                pair = jnp.concatenate([re[j : j + 1], im[j : j + 1]], axis=0)
                lattice[j, a, c] = pair.astype(BF16)


def finish_kernel(got, product, free, local, pseudo, rows):
    position = lax.axis_index("hist")
    size = rows.shape[0]
    total = got[0:size]
    for i in range(1, got.shape[0] // size):
        total = total + got[i * size : (i + 1) * size]
    scaled = total / total[:, 72:73]
    rows[...] = scaled
    mine = rows[pl.ds(position, 1), :]
    for a in range(3):
        for c in range(3):
            i = (a * 3 + c) * 8
            local[a, c] = jnp.concatenate([mine[:, i : i + 4], mine[:, i + 4 : i + 8]], axis=0)
    block = free.shape[0]
    lane = lax.broadcasted_iota(jnp.int32, (8, 128), 1)
    row = lax.broadcasted_iota(jnp.int32, (8, 128), 0) % 4
    low = low_half()
    real = [0.0] * block
    imag = [0.0] * block
    for t in range(size // 2):
        both = jnp.where(low, scaled[2 * t : 2 * t + 1], scaled[2 * t + 1 : 2 * t + 2])
        for a in range(3):
            re = jnp.sum(jnp.where(lane == row + 32 * a, both, 0.0), axis=1, keepdims=True)
            im = jnp.sum(jnp.where(lane == row + 32 * a + 4, both, 0.0), axis=1, keepdims=True)
            for j in range(block):
                x = product[a, j, 8 * t : 8 * t + 8, :]
                real[j] = real[j] + re * x
                imag[j] = imag[j] + im * x
    real = jnp.concatenate([jnp.sum(x, axis=0, keepdims=True) for x in real], axis=0)
    imag = jnp.concatenate([jnp.sum(x, axis=0, keepdims=True) for x in imag], axis=0)
    out = free[...] + real + signed_swap(imag)
    states = out.shape[1] // 2
    pseudo[0] = out[:, :states]
    pseudo[1] = out[:, states:]


VMEM = pl.BlockSpec(memory_space=pltpu.VMEM)
SMEM = pl.BlockSpec(memory_space=pltpu.SMEM)
HBM = pl.BlockSpec(memory_space=pltpu.HBM)


def grant(mib):
    return pltpu.CompilerParams(vmem_limit_bytes=mib << 20)


def per_device(
    step_index,
    band_energy,
    kernel_row,
    lattice_history,
    diagonal_inverse,
    multiplicity,
    state_energy,
    connection,
    predicted_row,
    pseudo_history,
):
    block, _, lanes = band_energy.shape
    states, flavours = connection.shape
    ka_size, hist_size = lax.axis_size("ka"), lax.axis_size("hist")
    chips = hist_size // 2
    everyone = ka_size * hist_size
    energy = jnp.transpose(band_energy, (1, 0, 2))
    sent = jax.ShapeDtypeStruct((chips, TERMS + INPUTS, lanes), BF16)

    own, other = pl.pallas_call(
        terms_kernel,
        out_shape=(sent, sent),
        in_specs=[SMEM, VMEM, VMEM, VMEM, VMEM, HBM],
        out_specs=(VMEM, VMEM),
        scratch_shapes=[
            pltpu.VMEM((block, 2, 3, 3, 8, lanes), F32),
            pltpu.VMEM((block, block * hist_size, 2 * states), F32),
            pltpu.VMEM(lattice_history.shape, BF16),
            pltpu.SemaphoreType.DMA((CHUNKS,)),
        ],
        compiler_params=grant(16),
        name="terms",
    )(
        step_index,
        jnp.transpose(kernel_row, (0, 2, 3, 1, 4)),
        energy,
        jnp.transpose(predicted_row, (0, 2, 1)),
        pseudo_history,
        lattice_history,
    )
    swapped = lax.ppermute(other, "hist", [(h, h ^ 1) for h in range(hist_size)])
    paired = pl.pallas_call(
        add_kernel,
        out_shape=jax.ShapeDtypeStruct((chips, TERMS + 2 * INPUTS, lanes), BF16),
        in_specs=[VMEM, VMEM],
        out_specs=VMEM,
        compiler_params=grant(8),
        name="add_pair",
    )(own, swapped)
    same_core = [[2 * t + c for t in range(chips)] for c in range(2)]
    arrived = lax.all_to_all(
        paired, "hist", split_axis=0, concat_axis=0, tiled=True, axis_index_groups=same_core
    )
    fresh, sums = pl.pallas_call(
        rows_kernel,
        out_shape=(
            jax.ShapeDtypeStruct((18, block, lanes), F32),
            jax.ShapeDtypeStruct((everyone, lanes), F32),
        ),
        in_specs=[SMEM, VMEM, VMEM, VMEM, VMEM],
        out_specs=(VMEM, VMEM),
        compiler_params=grant(8),
        name="rows",
    )(
        step_index,
        arrived,
        energy,
        jnp.transpose(diagonal_inverse, (1, 2, 0, 3)),
        multiplicity.reshape(1, lanes),
    )
    shared = lax.all_to_all(
        sums.reshape(everyone, 1, lanes), ("ka", "hist"), split_axis=0, concat_axis=0, tiled=True
    )
    product, free, lattice = pl.pallas_call(
        prepare_kernel,
        out_shape=(
            jax.ShapeDtypeStruct((3, block, block * hist_size, 2 * states), F32),
            jax.ShapeDtypeStruct((block, 2 * states), F32),
            jax.ShapeDtypeStruct((block, 3, 3, 2, lanes), BF16),
        ),
        in_specs=[SMEM, VMEM, VMEM, VMEM, VMEM],
        out_specs=(VMEM, VMEM, VMEM),
        scratch_shapes=[
            pltpu.VMEM((block * hist_size, 2 * states), F32),
            pltpu.VMEM((block * hist_size, 2 * states), F32),
            pltpu.VMEM((hist_size, 16, 2 * states), F32),
            pltpu.VMEM((3, 2, block * hist_size, 2 * states), F32),
        ],
        compiler_params=grant(8),
        cost_estimate=pl.CostEstimate(flops=40_000_000, bytes_accessed=2_000_000, transcendentals=2048),
        name="prepare",
    )(step_index, arrived, connection.T, state_energy.reshape(1, states), fresh)
    local, pseudo = pl.pallas_call(
        finish_kernel,
        out_shape=(
            jax.ShapeDtypeStruct((3, 3, 2, block), F32),
            jax.ShapeDtypeStruct((2, block, states), F32),
        ),
        in_specs=[VMEM, VMEM, VMEM],
        out_specs=(VMEM, VMEM),
        scratch_shapes=[pltpu.VMEM((hist_size, lanes), F32)],
        compiler_params=grant(8),
        name="finish",
    )(shared.reshape(everyone, lanes), product, free)
    return (
        jnp.transpose(lattice, (0, 3, 1, 2, 4)),
        jnp.transpose(local, (2, 0, 1, 3)),
        jnp.transpose(pseudo, (0, 2, 1)),
    )


def solution(mesh):
    in_specs = (
        P(),
        P("hist", None, "ka"),
        P("hist", None, None, None, "ka"),
        P("hist", None, None, None, None, "ka"),
        P(None, None, None, "ka"),
        P("ka"),
        P(),
        P(),
        P(None, None, "hist"),
        P("hist", None, None, None),
    )
    out_specs = (
        P("hist", None, None, None, "ka"),
        P(None, None, None, "hist"),
        P(None, None, "hist"),
    )
    return jax.shard_map(
        per_device, mesh=mesh, in_specs=in_specs, out_specs=out_specs, check_vma=False
    )
```

```python
import jax
import jax.numpy as jnp
from jax import lax
from jax.experimental import pallas as pl
from jax.experimental.pallas import tpu as pltpu
from jax.sharding import PartitionSpec as P

time_step = 0.05
coupling = 0.02
F32 = jnp.float32
BF16 = jnp.bfloat16
HIGHEST = lax.Precision.HIGHEST
TERMS = 80
CHUNKS = 4


def flag(condition):
    return jnp.where(condition, 1.0, 0.0).astype(F32)


def low_half(lanes=128):
    return lax.broadcasted_iota(jnp.int32, (8, lanes), 0) < 4


def high_low(x):
    high = x.astype(BF16).astype(F32)
    return jnp.where(low_half(x.shape[1]), high, x - high)


def interleave(p, q):
    low = low_half(p.shape[1])
    return jnp.where(low, p, pltpu.roll(q, 4, 0)), jnp.where(low, pltpu.roll(p, 4, 0), q)


def terms_kernel(
    step, kernel_row, energy, history, own, other, current_row, kernel_here, energy_here, coeff, store, few, sems
):
    position = lax.axis_index("hist")
    wide = history.shape[4] // CHUNKS

    def fetch(i):
        columns = pl.ds(pl.multiple_of(i * wide, wide), wide)
        return pltpu.make_async_copy(
            history.at[:, :, :, :, columns, :], store.at[:, :, :, :, columns, :], sems.at[i]
        )

    small = [
        pltpu.make_async_copy(kernel_row, kernel_here, few.at[0]),
        pltpu.make_async_copy(energy, energy_here, few.at[1]),
    ]
    for copy in small:
        copy.start()
    for i in range(CHUNKS):
        fetch(i).start()
    for copy in small:
        copy.wait()
    current = step[0]
    block = energy.shape[1]
    lanes = energy.shape[2]
    current_row[...] = jnp.full((1, lanes), current, jnp.int32)
    zero = jnp.zeros((1, lanes), F32)
    total = jnp.zeros((3, lanes), F32)
    for m in range(block):
        time = position * block + m
        weight = jnp.where(time < current, jnp.where(time == 0, 0.5, 1.0), 0.0).astype(F32)
        total = total + energy_here[:, m, :] * flag(time < current)
        for a in range(3):
            for b in range(3):
                rows = kernel_here[m, a, b].astype(F32) * weight
                for s in range(2):
                    coeff[m, s, a, b] = jnp.broadcast_to(rows[s : s + 1], (8, lanes))
    energies = high_low(jnp.concatenate([total, zero, total, zero], axis=0))
    even_core = position % 2 == 0

    def sixteen(start, pair):
        groups = [[], []]
        for c in range(3):
            acc = {}
            for m in range(block):
                for b in range(3):
                    columns = pl.ds(pl.multiple_of(start, 16), 16)
                    re = store[m, 0, b, c, columns, :].astype(F32)
                    im = store[m, 1, b, c, columns, :].astype(F32)
                    for a in range(3):
                        kr = coeff[m, 0, a, b]
                        ki = coeff[m, 1, a, b]
                        for g in range(2):
                            hr, hi = re[8 * g : 8 * g + 8], im[8 * g : 8 * g + 8]
                            x = kr * hr - ki * hi
                            y = kr * hi + ki * hr
                            acc[0, a, g] = x if m + b == 0 else acc[0, a, g] + x
                            acc[1, a, g] = y if m + b == 0 else acc[1, a, g] + y
            for g in range(2):
                groups[g] += [acc[s, a, g] for s in range(2) for a in range(3)]
        for g in range(2):
            chip = pair + g
            evens, odds = [], []

            def add(p, q):
                x, y = interleave(p, q)
                evens.append(x)
                odds.append(y)

            for u in range(9):
                add(groups[g][2 * u], groups[g][2 * u + 1])
            evens.append(energies * flag(position > 2 * chip))
            odds.append(energies * flag(position > 2 * chip + 1))
            even = jnp.concatenate(evens, axis=0).astype(BF16)
            odd = jnp.concatenate(odds, axis=0).astype(BF16)
            own[chip] = jnp.where(even_core, even, odd)
            other[chip] = jnp.where(even_core, odd, even)

    @pl.loop(0, CHUNKS)
    def _(i):
        fetch(i).wait()

        @pl.loop(0, wide // 16)
        def _(h):
            sixteen(i * wide + h * 16, i * (wide // 8) + 2 * h)


def add_kernel(own, arrived, out):
    @pl.loop(0, own.shape[0] // 4)
    def _(i):
        for u in range(4):
            t = 4 * i + u
            x = own[t].astype(F32) + arrived[t].astype(F32)
            energies = x[72:80]
            energies = high_low(energies + pltpu.roll(energies, 4, 0))
            out[t] = jnp.concatenate([x[:72], energies], axis=0).astype(BF16)


def signed_swap(x):
    lanes = x.shape[1]
    swapped = pltpu.roll(x, lanes // 2, 1)
    lower = lax.broadcasted_iota(jnp.int32, x.shape, 1) < lanes // 2
    return jnp.where(lower, -swapped, swapped)


def ahead_kernel(step, predicted, pseudo, links, levels, turned, reached, free):
    current, position = step[...], lax.axis_index("hist")
    block, states = predicted.shape[1], predicted.shape[2]
    for m in range(block):
        both = jnp.concatenate([pseudo[m, 0], pseudo[m, 1]], axis=0).astype(F32)
        turned[m] = both.T
    column = lax.broadcasted_iota(jnp.int32, (block, 2 * states), 0) + position * block
    weight = jnp.where(column < current, jnp.where(column == 0, 0.5, 1.0), 0.0) * coupling
    state = lax.broadcasted_iota(jnp.int32, (states, states), 0)
    for a in range(3):
        link = flag(links[2 * a : 2 * a + 1, :] == state) + flag(links[2 * a + 1 : 2 * a + 2, :] == state)
        link = jnp.concatenate([link, link], axis=1)
        for p in range(2):
            x = jnp.concatenate([predicted[p], predicted[p]], axis=0)
            x = jnp.dot(x, link, precision=HIGHEST, preferred_element_type=F32)
            reached[a, p] = x[:block] * weight.astype(F32)
    elapsed = (current - column).astype(F32)
    level = jnp.concatenate([levels[...], levels[...]], axis=1)
    spin = level * time_step * elapsed
    lower = lax.broadcasted_iota(jnp.int32, spin.shape, 1) < states
    free[...] = jnp.where(lower, -jnp.sin(spin), -jnp.cos(spin)) * (column <= current).astype(F32)


def rows_kernel(step, arrived, energy, inverse, multiplicity, turned, reached, fresh, own, other):
    current, position = step[...], lax.axis_index("hist")
    block = energy.shape[1]
    lanes = energy.shape[2]
    got = arrived[0].astype(F32)
    for i in range(1, arrived.shape[0]):
        got = got + arrived[i].astype(F32)
    later = got[72:75] + got[76:79]
    ends = []
    for m in reversed(range(block)):
        later = later + energy[:, m, :] * flag(position * block + m < current)
        ends.append(later)
    angle = jnp.concatenate(
        [ends[block - 1 - j][a : a + 1] for a in range(3) for j in range(block)], axis=0
    )
    angle = angle * time_step
    column = lax.broadcasted_iota(jnp.int32, angle.shape, 0) % block + position * block
    in_range = (column <= current).astype(F32)
    free = [-jnp.sin(angle) * in_range, -jnp.cos(angle) * in_range]

    def right(s, b, c):
        r = ((c * 2 + s) * 3 + b) * block
        x = got[r : r + block]
        return x + free[s][b * block : (b + 1) * block] if b == c else x

    entries = {}
    for c in range(3):
        side = {(s, b): right(s, b, c) for s in range(2) for b in range(3)}
        for a in range(3):
            re = im = 0.0
            for b in range(3):
                dr, di = inverse[a, b, 0:1, :], inverse[a, b, 1:2, :]
                re = re + dr * side[0, b] - di * side[1, b]
                im = im + dr * side[1, b] + di * side[0, b]
            entries[a, c, 0], entries[a, c, 1] = re, im
    entries = [entries[a, c, s] for a in range(3) for c in range(3) for s in range(2)]
    for i, x in enumerate(entries):
        fresh[i] = x
    shared = multiplicity[...].astype(F32)
    even_core = position % 2 == 0
    real = imag = 0.0
    for a in range(3):
        re = jnp.sum(entries[8 * a] * shared, axis=1, keepdims=True)
        im = jnp.sum(entries[8 * a + 1] * shared, axis=1, keepdims=True)
        real = real + re * reached[a, 0] - im * reached[a, 1]
        imag = imag + re * reached[a, 1] + im * reached[a, 0]
    entries += [jnp.ones((1, lanes), F32), jnp.zeros((lanes - 73, lanes), F32)]
    table = jnp.concatenate(entries, axis=0)
    weights = jnp.broadcast_to(shared, (8, lanes))
    message = lax.dot_general(
        weights, table, (((1,), (1,)), ((), ())), precision=HIGHEST, preferred_element_type=F32
    )[0:1]
    high = message.astype(BF16).astype(F32)
    message = jnp.concatenate([high, message - high], axis=0)
    for t in range(own.shape[0]):
        x = y = 0.0
        for m in range(block):
            past = turned[m, 8 * t : 8 * t + 8, :]
            x = x + real[m : m + 1] * past
            y = y + imag[m : m + 1] * past
        x = x + signed_swap(y)
        tile = []
        for core in range(2):
            pairs = [x[4 * core : 4 * core + 2], x[4 * core + 2 : 4 * core + 4]]
            pairs.append(message * flag(position == 2 * t + core))
            tile.append(jnp.concatenate(pairs, axis=1).astype(BF16))
        own[t] = jnp.where(even_core, tile[0], tile[1])
        other[t] = jnp.where(even_core, tile[1], tile[0])


def add_shares_kernel(own, arrived, out):
    for t in range(own.shape[0]):
        tile = (own[t].astype(F32) + arrived[t].astype(F32)).astype(BF16)
        for k in range(out.shape[0]):
            out[k, t] = tile


def lattice_kernel(fresh, lattice):
    for a in range(3):
        for c in range(3):
            i = (a * 3 + c) * 2
            re, im = fresh[i], fresh[i + 1]
            for j in range(lattice.shape[0]):
                pair = jnp.concatenate([re[j : j + 1], im[j : j + 1]], axis=0)
                lattice[j, a, c] = pair.astype(BF16)


def finish_kernel(got, free, local, pseudo):
    parts = []
    for i in range(4):
        x = got[i].astype(F32)
        for k in range(i + 4, got.shape[0], 4):
            x = x + got[k].astype(F32)
        parts.append(x)
    total = (parts[0] + parts[1]) + (parts[2] + parts[3])
    lanes = free.shape[1]
    states = lanes // 2
    sums = total[0:1, 2 * lanes :] + total[1:2, 2 * lanes :]
    count = sums[:, 72:73]
    mean = sums / count
    for a in range(3):
        for c in range(3):
            i = (a * 3 + c) * 8
            local[a, c] = jnp.concatenate([mean[:, i : i + 4], mean[:, i + 4 : i + 8]], axis=0)
    shares = jnp.concatenate([total[:, :lanes], total[:, lanes : 2 * lanes]], axis=0)
    out = free[...] + shares / count
    pseudo[0] = out[:, :states]
    pseudo[1] = out[:, states:]


VMEM = pl.BlockSpec(memory_space=pltpu.VMEM)
HBM = pl.BlockSpec(memory_space=pltpu.HBM)


def grant(mib):
    return pltpu.CompilerParams(vmem_limit_bytes=mib << 20)


def in_hbm(x):
    return pltpu.with_memory_space_constraint(x, pltpu.HBM)


def per_device(
    step_index,
    band_energy,
    kernel_row,
    lattice_history,
    diagonal_inverse,
    multiplicity,
    state_energy,
    connection,
    predicted_row,
    pseudo_history,
):
    block, _, lanes = band_energy.shape
    states, flavours = connection.shape
    ka_size, hist_size = lax.axis_size("ka"), lax.axis_size("hist")
    chips = hist_size // 2
    energy = jnp.transpose(band_energy, (1, 0, 2))
    kernel_pairs = jnp.transpose(kernel_row, (0, 2, 3, 1, 4))
    tiles = jax.ShapeDtypeStruct((chips, TERMS, lanes), BF16)
    cores = [(h, h ^ 1) for h in range(hist_size)]

    own, other, step = pl.pallas_call(
        terms_kernel,
        out_shape=(tiles, tiles, jax.ShapeDtypeStruct((1, lanes), jnp.int32)),
        in_specs=[pl.BlockSpec(memory_space=pltpu.SMEM), HBM, HBM, HBM],
        out_specs=(VMEM, VMEM, VMEM),
        scratch_shapes=[
            pltpu.VMEM(kernel_pairs.shape, BF16),
            pltpu.VMEM(energy.shape, F32),
            pltpu.VMEM((block, 2, 3, 3, 8, lanes), F32),
            pltpu.VMEM(lattice_history.shape, BF16),
            pltpu.SemaphoreType.DMA((2,)),
            pltpu.SemaphoreType.DMA((CHUNKS,)),
        ],
        compiler_params=grant(16),
        name="terms",
    )(step_index, in_hbm(kernel_pairs), in_hbm(energy), in_hbm(lattice_history))
    swapped = lax.ppermute(other, "hist", cores)
    paired = pl.pallas_call(
        add_kernel,
        out_shape=tiles,
        in_specs=[VMEM, VMEM],
        out_specs=VMEM,
        compiler_params=grant(8),
        name="add_pair",
    )(own, swapped)
    same_core = [[2 * t + c for t in range(chips)] for c in range(2)]
    arrived = lax.all_to_all(
        paired, "hist", split_axis=0, concat_axis=0, tiled=True, axis_index_groups=same_core
    )
    turned, reached, free = pl.pallas_call(
        ahead_kernel,
        out_shape=(
            jax.ShapeDtypeStruct((block, block * hist_size, 2 * states), F32),
            jax.ShapeDtypeStruct((3, 2, block, 2 * states), F32),
            jax.ShapeDtypeStruct((block, 2 * states), F32),
        ),
        in_specs=[VMEM, VMEM, VMEM, VMEM, VMEM],
        out_specs=(VMEM, VMEM, VMEM),
        compiler_params=grant(8),
        cost_estimate=pl.CostEstimate(flops=4_000_000, bytes_accessed=400_000, transcendentals=1024),
        name="ahead",
    )(
        step,
        jnp.transpose(predicted_row, (0, 2, 1)),
        pseudo_history,
        connection.T,
        state_energy.reshape(1, states),
    )
    shares = jax.ShapeDtypeStruct((chips, 2, 3 * lanes), BF16)
    fresh, own, other = pl.pallas_call(
        rows_kernel,
        out_shape=(jax.ShapeDtypeStruct((18, block, lanes), F32), shares, shares),
        in_specs=[VMEM, VMEM, VMEM, VMEM, VMEM, VMEM, VMEM],
        out_specs=(VMEM, VMEM, VMEM),
        compiler_params=grant(8),
        name="rows",
    )(
        step,
        arrived,
        energy,
        jnp.transpose(diagonal_inverse, (1, 2, 0, 3)),
        multiplicity.reshape(1, lanes),
        turned,
        reached,
    )
    swapped = lax.ppermute(other, "hist", cores)
    paired = pl.pallas_call(
        add_shares_kernel,
        out_shape=jax.ShapeDtypeStruct((ka_size, *shares.shape), BF16),
        in_specs=[VMEM, VMEM],
        out_specs=VMEM,
        compiler_params=grant(8),
        name="add_shares",
    )(own, swapped)
    same_core = [
        [k * hist_size + 2 * t + c for k in range(ka_size) for t in range(chips)] for c in range(2)
    ]
    got = lax.all_to_all(
        paired.reshape(ka_size * chips, 2, 3 * lanes),
        ("ka", "hist"),
        split_axis=0,
        concat_axis=0,
        tiled=True,
        axis_index_groups=same_core,
    )
    lattice = pl.pallas_call(
        lattice_kernel,
        out_shape=jax.ShapeDtypeStruct((block, 3, 3, 2, lanes), BF16),
        in_specs=[VMEM],
        out_specs=VMEM,
        compiler_params=grant(8),
        cost_estimate=pl.CostEstimate(flops=10_000, bytes_accessed=60_000, transcendentals=0),
        name="lattice",
    )(fresh)
    local, pseudo = pl.pallas_call(
        finish_kernel,
        out_shape=(
            jax.ShapeDtypeStruct((3, 3, 2, block), F32),
            jax.ShapeDtypeStruct((2, block, states), F32),
        ),
        in_specs=[VMEM, VMEM],
        out_specs=(VMEM, VMEM),
        compiler_params=grant(8),
        name="finish",
    )(got, free)
    return (
        jnp.transpose(lattice, (0, 3, 1, 2, 4)),
        jnp.transpose(local, (2, 0, 1, 3)),
        jnp.transpose(pseudo, (0, 2, 1)),
    )


def solution(mesh):
    in_specs = (
        P(),
        P("hist", None, "ka"),
        P("hist", None, None, None, "ka"),
        P("hist", None, None, None, None, "ka"),
        P(None, None, None, "ka"),
        P("ka"),
        P(),
        P(),
        P(None, None, "hist"),
        P("hist", None, None, None),
    )
    out_specs = (
        P("hist", None, None, None, "ka"),
        P(None, None, None, "hist"),
        P(None, None, "hist"),
    )
    return jax.shard_map(
        per_device, mesh=mesh, in_specs=in_specs, out_specs=out_specs, check_vma=False
    )
```

```python
import jax
import jax.numpy as jnp
from jax import lax
from jax.experimental import pallas as pl
from jax.experimental.pallas import tpu as pltpu
from jax.sharding import PartitionSpec as P

time_step = 0.05
coupling = 0.02
F32 = jnp.float32
BF16 = jnp.bfloat16
HIGHEST = lax.Precision.HIGHEST
TERMS = 80
CHUNKS = 4


def flag(condition):
    return jnp.where(condition, 1.0, 0.0).astype(F32)


def low_half(lanes=128):
    return lax.broadcasted_iota(jnp.int32, (8, lanes), 0) < 4


def high_low(x):
    high = x.astype(BF16).astype(F32)
    return jnp.where(low_half(x.shape[1]), high, x - high)


def interleave(p, q):
    low = low_half(p.shape[1])
    return jnp.where(low, p, pltpu.roll(q, 4, 0)), jnp.where(low, pltpu.roll(p, 4, 0), q)


def terms_kernel(
    step, kernel_row, energy, history, own, other, current_row, kernel_here, energy_here, coeff, store, few, sems
):
    position = lax.axis_index("hist")
    wide = history.shape[4] // CHUNKS

    def fetch(i):
        columns = pl.ds(pl.multiple_of(i * wide, wide), wide)
        return pltpu.make_async_copy(
            history.at[:, :, :, :, columns, :], store.at[:, :, :, :, columns, :], sems.at[i]
        )

    small = [
        pltpu.make_async_copy(kernel_row, kernel_here, few.at[0]),
        pltpu.make_async_copy(energy, energy_here, few.at[1]),
    ]
    for copy in small:
        copy.start()
    for i in range(CHUNKS):
        fetch(i).start()
    for copy in small:
        copy.wait()
    current = step[0]
    block = energy.shape[1]
    lanes = energy.shape[2]
    current_row[...] = jnp.full((1, lanes), current, jnp.int32)
    zero = jnp.zeros((1, lanes), F32)
    total = jnp.zeros((3, lanes), F32)
    for m in range(block):
        time = position * block + m
        weight = jnp.where(time < current, jnp.where(time == 0, 0.5, 1.0), 0.0).astype(F32)
        total = total + energy_here[:, m, :] * flag(time < current)
        for a in range(3):
            for b in range(3):
                rows = kernel_here[m, a, b].astype(F32) * weight
                re, im = rows[0:1], rows[1:2]
                for i, x in enumerate((re, re + im, im - re)):
                    coeff[m, i, a, b] = jnp.broadcast_to(x, (8, lanes))
    energies = high_low(jnp.concatenate([total, zero, total, zero], axis=0))
    even_core = position % 2 == 0

    def sixteen(start, pair):
        groups = [[], []]
        for c in range(3):
            acc = {}
            for m in range(block):
                for b in range(3):
                    columns = pl.ds(pl.multiple_of(start, 16), 16)
                    re = store[m, 0, b, c, columns, :].astype(F32)
                    im = store[m, 1, b, c, columns, :].astype(F32)
                    both = re + im
                    for a in range(3):
                        weights = [coeff[m, i, a, b] for i in range(3)]
                        for g in range(2):
                            rows = slice(8 * g, 8 * g + 8)
                            for i, x in enumerate((both, im, re)):
                                x = weights[i] * x[rows]
                                acc[i, a, g] = x if m + b == 0 else acc[i, a, g] + x
            for a in range(3):
                for g in range(2):
                    x = acc[0, a, g]
                    acc[0, a, g], acc[1, a, g] = x - acc[1, a, g], x + acc[2, a, g]
            for g in range(2):
                groups[g] += [acc[s, a, g] for s in range(2) for a in range(3)]
        for g in range(2):
            chip = pair + g
            evens, odds = [], []

            def add(p, q):
                x, y = interleave(p, q)
                evens.append(x)
                odds.append(y)

            for u in range(9):
                add(groups[g][2 * u], groups[g][2 * u + 1])
            evens.append(energies * flag(position > 2 * chip))
            odds.append(energies * flag(position > 2 * chip + 1))
            even = jnp.concatenate(evens, axis=0).astype(BF16)
            odd = jnp.concatenate(odds, axis=0).astype(BF16)
            own[chip] = jnp.where(even_core, even, odd)
            other[chip] = jnp.where(even_core, odd, even)

    @pl.loop(0, CHUNKS)
    def _(i):
        fetch(i).wait()

        @pl.loop(0, wide // 16)
        def _(h):
            sixteen(i * wide + h * 16, i * (wide // 8) + 2 * h)


def add_kernel(own, arrived, _, out):
    @pl.loop(0, own.shape[0] // 4)
    def _(i):
        for u in range(4):
            t = 4 * i + u
            x = own[t].astype(F32) + arrived[t].astype(F32)
            energies = x[72:80]
            energies = high_low(energies + pltpu.roll(energies, 4, 0))
            out[t] = jnp.concatenate([x[:72], energies], axis=0).astype(BF16)


def signed_swap(x):
    lanes = x.shape[1]
    swapped = pltpu.roll(x, lanes // 2, 1)
    lower = lax.broadcasted_iota(jnp.int32, x.shape, 1) < lanes // 2
    return jnp.where(lower, -swapped, swapped)


def ahead_kernel(step, predicted, pseudo, links, levels, turned, reached, free):
    current, position = step[...], lax.axis_index("hist")
    block, states = predicted.shape[1], predicted.shape[2]
    for m in range(block):
        both = jnp.concatenate([pseudo[m, 0], pseudo[m, 1]], axis=0).astype(F32)
        turned[m] = both.T
    column = lax.broadcasted_iota(jnp.int32, (block, 2 * states), 0) + position * block
    weight = jnp.where(column < current, jnp.where(column == 0, 0.5, 1.0), 0.0) * coupling
    state = lax.broadcasted_iota(jnp.int32, (states, states), 0)
    for a in range(3):
        link = flag(links[2 * a : 2 * a + 1, :] == state) + flag(links[2 * a + 1 : 2 * a + 2, :] == state)
        link = jnp.concatenate([link, link], axis=1)
        for p in range(2):
            x = jnp.concatenate([predicted[p], predicted[p]], axis=0)
            x = jnp.dot(x, link, precision=HIGHEST, preferred_element_type=F32)
            reached[a, p] = x[:block] * weight.astype(F32)
    elapsed = (current - column).astype(F32)
    level = jnp.concatenate([levels[...], levels[...]], axis=1)
    spin = level * time_step * elapsed
    lower = lax.broadcasted_iota(jnp.int32, spin.shape, 1) < states
    free[...] = jnp.where(lower, -jnp.sin(spin), -jnp.cos(spin)) * (column <= current).astype(F32)


def rows_kernel(step, arrived, energy, inverse, multiplicity, turned, reached, fresh, own, other):
    current, position = step[...], lax.axis_index("hist")
    block = energy.shape[1]
    lanes = energy.shape[2]
    got = arrived[0].astype(F32)
    for i in range(1, arrived.shape[0]):
        got = got + arrived[i].astype(F32)
    later = got[72:75] + got[76:79]
    ends = []
    for m in reversed(range(block)):
        later = later + energy[:, m, :] * flag(position * block + m < current)
        ends.append(later)
    angle = jnp.concatenate(
        [ends[block - 1 - j][a : a + 1] for a in range(3) for j in range(block)], axis=0
    )
    angle = angle * time_step
    column = lax.broadcasted_iota(jnp.int32, angle.shape, 0) % block + position * block
    in_range = (column <= current).astype(F32)
    free = [-jnp.sin(angle) * in_range, -jnp.cos(angle) * in_range]

    def right(s, b, c):
        r = ((c * 2 + s) * 3 + b) * block
        x = got[r : r + block]
        return x + free[s][b * block : (b + 1) * block] if b == c else x

    entries = {}
    for c in range(3):
        side = {(s, b): right(s, b, c) for s in range(2) for b in range(3)}
        for a in range(3):
            re = im = 0.0
            for b in range(3):
                dr, di = inverse[a, b, 0:1, :], inverse[a, b, 1:2, :]
                re = re + dr * side[0, b] - di * side[1, b]
                im = im + dr * side[1, b] + di * side[0, b]
            entries[a, c, 0], entries[a, c, 1] = re, im
    entries = [entries[a, c, s] for a in range(3) for c in range(3) for s in range(2)]
    for i, x in enumerate(entries):
        fresh[i] = x
    shared = multiplicity[...].astype(F32)
    even_core = position % 2 == 0
    real = imag = 0.0
    for a in range(3):
        re = jnp.sum(entries[8 * a] * shared, axis=1, keepdims=True)
        im = jnp.sum(entries[8 * a + 1] * shared, axis=1, keepdims=True)
        real = real + re * reached[a, 0] - im * reached[a, 1]
        imag = imag + re * reached[a, 1] + im * reached[a, 0]
    entries += [jnp.ones((1, lanes), F32), jnp.zeros((lanes - 73, lanes), F32)]
    table = jnp.concatenate(entries, axis=0)
    weights = jnp.broadcast_to(shared, (8, lanes))
    message = lax.dot_general(
        weights, table, (((1,), (1,)), ((), ())), precision=HIGHEST, preferred_element_type=F32
    )[0:1]
    high = message.astype(BF16).astype(F32)
    message = jnp.concatenate([high, message - high], axis=0)
    for t in range(own.shape[0]):
        x = y = 0.0
        for m in range(block):
            past = turned[m, 8 * t : 8 * t + 8, :]
            x = x + real[m : m + 1] * past
            y = y + imag[m : m + 1] * past
        x = x + signed_swap(y)
        tile = []
        for core in range(2):
            pairs = [x[4 * core : 4 * core + 2], x[4 * core + 2 : 4 * core + 4]]
            pairs.append(message * flag(position == 2 * t + core))
            tile.append(jnp.concatenate(pairs, axis=1).astype(BF16))
        own[t] = jnp.where(even_core, tile[0], tile[1])
        other[t] = jnp.where(even_core, tile[1], tile[0])


def add_shares_kernel(own, arrived, _, out):
    for t in range(own.shape[0]):
        tile = (own[t].astype(F32) + arrived[t].astype(F32)).astype(BF16)
        for k in range(out.shape[0]):
            out[k, t] = tile


def lattice_kernel(fresh, lattice, written):
    written[...] = fresh[0, 0:1]
    for a in range(3):
        for c in range(3):
            i = (a * 3 + c) * 2
            re, im = fresh[i], fresh[i + 1]
            for j in range(lattice.shape[0]):
                pair = jnp.concatenate([re[j : j + 1], im[j : j + 1]], axis=0)
                lattice[j, a, c] = pair.astype(BF16)


def finish_kernel(got, free, local, pseudo):
    parts = []
    for i in range(4):
        x = got[i].astype(F32)
        for k in range(i + 4, got.shape[0], 4):
            x = x + got[k].astype(F32)
        parts.append(x)
    total = (parts[0] + parts[1]) + (parts[2] + parts[3])
    lanes = free.shape[1]
    states = lanes // 2
    sums = total[0:1, 2 * lanes :] + total[1:2, 2 * lanes :]
    count = sums[:, 72:73]
    mean = sums / count
    for a in range(3):
        for c in range(3):
            i = (a * 3 + c) * 8
            local[a, c] = jnp.concatenate([mean[:, i : i + 4], mean[:, i + 4 : i + 8]], axis=0)
    shares = jnp.concatenate([total[:, :lanes], total[:, lanes : 2 * lanes]], axis=0)
    out = free[...] + shares / count
    pseudo[0] = out[:, :states]
    pseudo[1] = out[:, states:]


VMEM = pl.BlockSpec(memory_space=pltpu.VMEM)
HBM = pl.BlockSpec(memory_space=pltpu.HBM)
ANY = pl.BlockSpec(memory_space=pl.ANY)


def grant(mib):
    return pltpu.CompilerParams(vmem_limit_bytes=mib << 20)


def in_hbm(x):
    return pltpu.with_memory_space_constraint(x, pltpu.HBM)


def per_device(
    step_index,
    band_energy,
    kernel_row,
    lattice_history,
    diagonal_inverse,
    multiplicity,
    state_energy,
    connection,
    predicted_row,
    pseudo_history,
):
    block, _, lanes = band_energy.shape
    states, flavours = connection.shape
    ka_size, hist_size = lax.axis_size("ka"), lax.axis_size("hist")
    chips = hist_size // 2
    energy = jnp.transpose(band_energy, (1, 0, 2))
    kernel_pairs = jnp.transpose(kernel_row, (0, 2, 3, 1, 4))
    tiles = jax.ShapeDtypeStruct((chips, TERMS, lanes), BF16)
    cores = [(h, h ^ 1) for h in range(hist_size)]

    own, other, step = pl.pallas_call(
        terms_kernel,
        out_shape=(tiles, tiles, jax.ShapeDtypeStruct((1, lanes), jnp.int32)),
        in_specs=[pl.BlockSpec(memory_space=pltpu.SMEM), HBM, HBM, HBM],
        out_specs=(VMEM, VMEM, VMEM),
        scratch_shapes=[
            pltpu.VMEM(kernel_pairs.shape, BF16),
            pltpu.VMEM(energy.shape, F32),
            pltpu.VMEM((block, 3, 3, 3, 8, lanes), F32),
            pltpu.VMEM(lattice_history.shape, BF16),
            pltpu.SemaphoreType.DMA((2,)),
            pltpu.SemaphoreType.DMA((CHUNKS,)),
        ],
        compiler_params=grant(16),
        name="terms",
    )(step_index, in_hbm(kernel_pairs), in_hbm(energy), in_hbm(lattice_history))
    swapped = lax.ppermute(other, "hist", cores)
    turned, reached, free = pl.pallas_call(
        ahead_kernel,
        out_shape=(
            jax.ShapeDtypeStruct((block, block * hist_size, 2 * states), F32),
            jax.ShapeDtypeStruct((3, 2, block, 2 * states), F32),
            jax.ShapeDtypeStruct((block, 2 * states), F32),
        ),
        in_specs=[VMEM, VMEM, VMEM, VMEM, VMEM],
        out_specs=(VMEM, VMEM, VMEM),
        compiler_params=grant(8),
        cost_estimate=pl.CostEstimate(flops=4_000_000, bytes_accessed=400_000, transcendentals=1024),
        name="ahead",
    )(
        step,
        jnp.transpose(predicted_row, (0, 2, 1)),
        pseudo_history,
        connection.T,
        state_energy.reshape(1, states),
    )
    paired = pl.pallas_call(
        add_kernel,
        out_shape=tiles,
        in_specs=[VMEM, VMEM, ANY],
        out_specs=VMEM,
        compiler_params=grant(8),
        name="add_pair",
    )(own, swapped, free)
    same_core = [[2 * t + c for t in range(chips)] for c in range(2)]
    arrived = lax.all_to_all(
        paired, "hist", split_axis=0, concat_axis=0, tiled=True, axis_index_groups=same_core
    )
    shares = jax.ShapeDtypeStruct((chips, 2, 3 * lanes), BF16)
    fresh, own, other = pl.pallas_call(
        rows_kernel,
        out_shape=(jax.ShapeDtypeStruct((18, block, lanes), F32), shares, shares),
        in_specs=[VMEM, VMEM, VMEM, VMEM, VMEM, VMEM, VMEM],
        out_specs=(VMEM, VMEM, VMEM),
        compiler_params=grant(8),
        name="rows",
    )(
        step,
        arrived,
        energy,
        jnp.transpose(diagonal_inverse, (1, 2, 0, 3)),
        multiplicity.reshape(1, lanes),
        turned,
        reached,
    )
    swapped = lax.ppermute(other, "hist", cores)
    lattice, written = pl.pallas_call(
        lattice_kernel,
        out_shape=(
            jax.ShapeDtypeStruct((block, 3, 3, 2, lanes), BF16),
            jax.ShapeDtypeStruct((1, lanes), F32),
        ),
        in_specs=[VMEM],
        out_specs=(VMEM, VMEM),
        compiler_params=grant(8),
        cost_estimate=pl.CostEstimate(flops=10_000, bytes_accessed=60_000, transcendentals=0),
        name="lattice",
    )(fresh)
    paired = pl.pallas_call(
        add_shares_kernel,
        out_shape=jax.ShapeDtypeStruct((ka_size, *shares.shape), BF16),
        in_specs=[VMEM, VMEM, ANY],
        out_specs=VMEM,
        compiler_params=grant(8),
        name="add_shares",
    )(own, swapped, written)
    same_core = [
        [k * hist_size + 2 * t + c for k in range(ka_size) for t in range(chips)] for c in range(2)
    ]
    got = lax.all_to_all(
        paired.reshape(ka_size * chips, 2, 3 * lanes),
        ("ka", "hist"),
        split_axis=0,
        concat_axis=0,
        tiled=True,
        axis_index_groups=same_core,
    )
    local, pseudo = pl.pallas_call(
        finish_kernel,
        out_shape=(
            jax.ShapeDtypeStruct((3, 3, 2, block), F32),
            jax.ShapeDtypeStruct((2, block, states), F32),
        ),
        in_specs=[VMEM, VMEM],
        out_specs=(VMEM, VMEM),
        compiler_params=grant(8),
        name="finish",
    )(got, free)
    return (
        jnp.transpose(lattice, (0, 3, 1, 2, 4)),
        jnp.transpose(local, (2, 0, 1, 3)),
        jnp.transpose(pseudo, (0, 2, 1)),
    )


def solution(mesh):
    in_specs = (
        P(),
        P("hist", None, "ka"),
        P("hist", None, None, None, "ka"),
        P("hist", None, None, None, None, "ka"),
        P(None, None, None, "ka"),
        P("ka"),
        P(),
        P(),
        P(None, None, "hist"),
        P("hist", None, None, None),
    )
    out_specs = (
        P("hist", None, None, None, "ka"),
        P(None, None, None, "hist"),
        P(None, None, "hist"),
    )
    return jax.shard_map(
        per_device, mesh=mesh, in_specs=in_specs, out_specs=out_specs, check_vma=False
    )
```

```python
import jax
import jax.numpy as jnp
from jax import lax
from jax.experimental import pallas as pl
from jax.experimental.pallas import tpu as pltpu
from jax.sharding import PartitionSpec as P

time_step = 0.05
coupling = 0.02
F32 = jnp.float32
BF16 = jnp.bfloat16
HIGHEST = lax.Precision.HIGHEST
TERMS = 80
CHUNKS = 4


def slot_of(chip, chips):
    half = chips // 2
    return lax.rem(chip, half) * 2 + lax.div(chip, half)


def spread(chips):
    half = chips // 2
    bits = half.bit_length() - 1
    order = [sum((i >> b & 1) << (bits - 1 - b) for b in range(bits)) for i in range(half)]
    return [h * half + i for i in order for h in range(2)]


def flag(condition):
    return jnp.where(condition, 1.0, 0.0).astype(F32)


def low_half(lanes=128):
    return lax.broadcasted_iota(jnp.int32, (8, lanes), 0) < 4


def high_low(x):
    high = x.astype(BF16).astype(F32)
    return jnp.where(low_half(x.shape[1]), high, x - high)


def interleave(p, q):
    low = low_half(p.shape[1])
    return jnp.where(low, p, pltpu.roll(q, 4, 0)), jnp.where(low, pltpu.roll(p, 4, 0), q)


def terms_kernel(
    step, kernel_row, energy, history, own, other, current_row, kernel_here, energy_here, coeff, store, few, sems
):
    position = lax.axis_index("hist")
    wide = history.shape[4] // CHUNKS

    def fetch(i):
        columns = pl.ds(pl.multiple_of(i * wide, wide), wide)
        return pltpu.make_async_copy(
            history.at[:, :, :, :, columns, :], store.at[:, :, :, :, columns, :], sems.at[i]
        )

    small = [
        pltpu.make_async_copy(kernel_row, kernel_here, few.at[0]),
        pltpu.make_async_copy(energy, energy_here, few.at[1]),
    ]
    for copy in small:
        copy.start()
    for i in range(CHUNKS):
        fetch(i).start()
    for copy in small:
        copy.wait()
    current = step[0]
    block = energy.shape[1]
    lanes = energy.shape[2]
    current_row[...] = jnp.full((1, lanes), current, jnp.int32)
    zero = jnp.zeros((1, lanes), F32)
    total = jnp.zeros((3, lanes), F32)
    for m in range(block):
        time = position * block + m
        weight = jnp.where(time < current, jnp.where(time == 0, 0.5, 1.0), 0.0).astype(F32)
        total = total + energy_here[:, m, :] * flag(time < current)
        for a in range(3):
            for b in range(3):
                rows = kernel_here[m, a, b].astype(F32) * weight
                re, im = rows[0:1], rows[1:2]
                for i, x in enumerate((re, re + im, im - re)):
                    coeff[m, i, a, b] = jnp.broadcast_to(x, (8, lanes))
    energies = high_low(jnp.concatenate([total, zero, total, zero], axis=0))
    even_core = position % 2 == 0

    def sixteen(start, pair):
        groups = [[], []]
        for c in range(3):
            acc = {}
            for m in range(block):
                for b in range(3):
                    columns = pl.ds(pl.multiple_of(start, 16), 16)
                    re = store[m, 0, b, c, columns, :].astype(F32)
                    im = store[m, 1, b, c, columns, :].astype(F32)
                    both = re + im
                    for a in range(3):
                        weights = [coeff[m, i, a, b] for i in range(3)]
                        for g in range(2):
                            rows = slice(8 * g, 8 * g + 8)
                            for i, x in enumerate((both, im, re)):
                                x = weights[i] * x[rows]
                                acc[i, a, g] = x if m + b == 0 else acc[i, a, g] + x
            for a in range(3):
                for g in range(2):
                    x = acc[0, a, g]
                    acc[0, a, g], acc[1, a, g] = x - acc[1, a, g], x + acc[2, a, g]
            for g in range(2):
                groups[g] += [acc[s, a, g] for s in range(2) for a in range(3)]
        for g in range(2):
            chip = pair + g
            evens, odds = [], []

            def add(p, q):
                x, y = interleave(p, q)
                evens.append(x)
                odds.append(y)

            for u in range(9):
                add(groups[g][2 * u], groups[g][2 * u + 1])
            evens.append(energies * flag(position > 2 * chip))
            odds.append(energies * flag(position > 2 * chip + 1))
            even = jnp.concatenate(evens, axis=0).astype(BF16)
            odd = jnp.concatenate(odds, axis=0).astype(BF16)
            slot = slot_of(chip, own.shape[0])
            own[slot] = jnp.where(even_core, even, odd)
            other[slot] = jnp.where(even_core, odd, even)

    @pl.loop(0, CHUNKS)
    def _(i):
        fetch(i).wait()

        @pl.loop(0, wide // 16)
        def _(h):
            sixteen(i * wide + h * 16, i * (wide // 8) + 2 * h)


def add_kernel(own, arrived, _, out):
    @pl.loop(0, own.shape[0] // 4)
    def _(i):
        for u in range(4):
            t = 4 * i + u
            x = own[t].astype(F32) + arrived[t].astype(F32)
            energies = x[72:80]
            energies = high_low(energies + pltpu.roll(energies, 4, 0))
            out[t] = jnp.concatenate([x[:72], energies], axis=0).astype(BF16)


def signed_swap(x):
    lanes = x.shape[1]
    swapped = pltpu.roll(x, lanes // 2, 1)
    lower = lax.broadcasted_iota(jnp.int32, x.shape, 1) < lanes // 2
    return jnp.where(lower, -swapped, swapped)


def ahead_kernel(step, predicted, pseudo, links, levels, turned, reached, free):
    current, position = step[...], lax.axis_index("hist")
    block, states = predicted.shape[1], predicted.shape[2]
    for m in range(block):
        both = jnp.concatenate([pseudo[m, 0], pseudo[m, 1]], axis=0).astype(F32)
        turned[m] = both.T
    column = lax.broadcasted_iota(jnp.int32, (block, 2 * states), 0) + position * block
    weight = jnp.where(column < current, jnp.where(column == 0, 0.5, 1.0), 0.0) * coupling
    state = lax.broadcasted_iota(jnp.int32, (states, states), 0)
    for a in range(3):
        link = flag(links[2 * a : 2 * a + 1, :] == state) + flag(links[2 * a + 1 : 2 * a + 2, :] == state)
        link = jnp.concatenate([link, link], axis=1)
        for p in range(2):
            x = jnp.concatenate([predicted[p], predicted[p]], axis=0)
            x = jnp.dot(x, link, precision=HIGHEST, preferred_element_type=F32)
            reached[a, p] = x[:block] * weight.astype(F32)
    elapsed = (current - column).astype(F32)
    level = jnp.concatenate([levels[...], levels[...]], axis=1)
    spin = level * time_step * elapsed
    lower = lax.broadcasted_iota(jnp.int32, spin.shape, 1) < states
    free[...] = jnp.where(lower, -jnp.sin(spin), -jnp.cos(spin)) * (column <= current).astype(F32)


def rows_kernel(step, arrived, energy, inverse, multiplicity, turned, reached, fresh, own, other):
    current, position = step[...], lax.axis_index("hist")
    block = energy.shape[1]
    lanes = energy.shape[2]
    got = arrived[0].astype(F32)
    for i in range(1, arrived.shape[0]):
        got = got + arrived[i].astype(F32)
    later = got[72:75] + got[76:79]
    ends = []
    for m in reversed(range(block)):
        later = later + energy[:, m, :] * flag(position * block + m < current)
        ends.append(later)
    angle = jnp.concatenate(
        [ends[block - 1 - j][a : a + 1] for a in range(3) for j in range(block)], axis=0
    )
    angle = angle * time_step
    column = lax.broadcasted_iota(jnp.int32, angle.shape, 0) % block + position * block
    in_range = (column <= current).astype(F32)
    free = [-jnp.sin(angle) * in_range, -jnp.cos(angle) * in_range]

    def right(s, b, c):
        r = ((c * 2 + s) * 3 + b) * block
        x = got[r : r + block]
        return x + free[s][b * block : (b + 1) * block] if b == c else x

    entries = {}
    for c in range(3):
        side = {(s, b): right(s, b, c) for s in range(2) for b in range(3)}
        for a in range(3):
            re = im = 0.0
            for b in range(3):
                dr, di = inverse[a, b, 0:1, :], inverse[a, b, 1:2, :]
                re = re + dr * side[0, b] - di * side[1, b]
                im = im + dr * side[1, b] + di * side[0, b]
            entries[a, c, 0], entries[a, c, 1] = re, im
    entries = [entries[a, c, s] for a in range(3) for c in range(3) for s in range(2)]
    for i, x in enumerate(entries):
        fresh[i] = x
    shared = multiplicity[...].astype(F32)
    even_core = position % 2 == 0
    real = imag = 0.0
    for a in range(3):
        re = jnp.sum(entries[8 * a] * shared, axis=1, keepdims=True)
        im = jnp.sum(entries[8 * a + 1] * shared, axis=1, keepdims=True)
        real = real + re * reached[a, 0] - im * reached[a, 1]
        imag = imag + re * reached[a, 1] + im * reached[a, 0]
    entries += [jnp.ones((1, lanes), F32), jnp.zeros((lanes - 73, lanes), F32)]
    table = jnp.concatenate(entries, axis=0)
    weights = jnp.broadcast_to(shared, (8, lanes))
    message = lax.dot_general(
        weights, table, (((1,), (1,)), ((), ())), precision=HIGHEST, preferred_element_type=F32
    )[0:1]
    high = message.astype(BF16).astype(F32)
    message = jnp.concatenate([high, message - high], axis=0)
    for t in range(own.shape[0]):
        x = y = 0.0
        for m in range(block):
            past = turned[m, 8 * t : 8 * t + 8, :]
            x = x + real[m : m + 1] * past
            y = y + imag[m : m + 1] * past
        x = x + signed_swap(y)
        tile = []
        for core in range(2):
            pairs = [x[4 * core : 4 * core + 2], x[4 * core + 2 : 4 * core + 4]]
            pairs.append(message * flag(position == 2 * t + core))
            tile.append(jnp.concatenate(pairs, axis=1).astype(BF16))
        own[t] = jnp.where(even_core, tile[0], tile[1])
        other[t] = jnp.where(even_core, tile[1], tile[0])


def add_shares_kernel(own, arrived, _, out):
    for i, t in enumerate(spread(own.shape[0])):
        tile = (own[t].astype(F32) + arrived[t].astype(F32)).astype(BF16)
        for k in range(out.shape[1]):
            out[i, k] = tile


def lattice_kernel(fresh, lattice, written):
    written[...] = fresh[0, 0:1]
    for a in range(3):
        for c in range(3):
            i = (a * 3 + c) * 2
            re, im = fresh[i], fresh[i + 1]
            for j in range(lattice.shape[0]):
                pair = jnp.concatenate([re[j : j + 1], im[j : j + 1]], axis=0)
                lattice[j, a, c] = pair.astype(BF16)


def finish_kernel(got, free, local, pseudo):
    parts = []
    for i in range(4):
        x = got[i].astype(F32)
        for k in range(i + 4, got.shape[0], 4):
            x = x + got[k].astype(F32)
        parts.append(x)
    total = (parts[0] + parts[1]) + (parts[2] + parts[3])
    lanes = free.shape[1]
    states = lanes // 2
    sums = total[0:1, 2 * lanes :] + total[1:2, 2 * lanes :]
    count = sums[:, 72:73]
    mean = sums / count
    for a in range(3):
        for c in range(3):
            i = (a * 3 + c) * 8
            local[a, c] = jnp.concatenate([mean[:, i : i + 4], mean[:, i + 4 : i + 8]], axis=0)
    shares = jnp.concatenate([total[:, :lanes], total[:, lanes : 2 * lanes]], axis=0)
    out = free[...] + shares / count
    pseudo[0] = out[:, :states]
    pseudo[1] = out[:, states:]


VMEM = pl.BlockSpec(memory_space=pltpu.VMEM)
HBM = pl.BlockSpec(memory_space=pltpu.HBM)
ANY = pl.BlockSpec(memory_space=pl.ANY)


def grant(mib):
    return pltpu.CompilerParams(vmem_limit_bytes=mib << 20)


def in_hbm(x):
    return pltpu.with_memory_space_constraint(x, pltpu.HBM)


def per_device(
    step_index,
    band_energy,
    kernel_row,
    lattice_history,
    diagonal_inverse,
    multiplicity,
    state_energy,
    connection,
    predicted_row,
    pseudo_history,
):
    block, _, lanes = band_energy.shape
    states, flavours = connection.shape
    ka_size, hist_size = lax.axis_size("ka"), lax.axis_size("hist")
    chips = hist_size // 2
    energy = jnp.transpose(band_energy, (1, 0, 2))
    kernel_pairs = jnp.transpose(kernel_row, (0, 2, 3, 1, 4))
    tiles = jax.ShapeDtypeStruct((chips, TERMS, lanes), BF16)
    cores = [(h, h ^ 1) for h in range(hist_size)]

    own, other, step = pl.pallas_call(
        terms_kernel,
        out_shape=(tiles, tiles, jax.ShapeDtypeStruct((1, lanes), jnp.int32)),
        in_specs=[pl.BlockSpec(memory_space=pltpu.SMEM), HBM, HBM, HBM],
        out_specs=(VMEM, VMEM, VMEM),
        scratch_shapes=[
            pltpu.VMEM(kernel_pairs.shape, BF16),
            pltpu.VMEM(energy.shape, F32),
            pltpu.VMEM((block, 3, 3, 3, 8, lanes), F32),
            pltpu.VMEM(lattice_history.shape, BF16),
            pltpu.SemaphoreType.DMA((2,)),
            pltpu.SemaphoreType.DMA((CHUNKS,)),
        ],
        compiler_params=grant(16),
        name="terms",
    )(step_index, in_hbm(kernel_pairs), in_hbm(energy), in_hbm(lattice_history))
    swapped = lax.ppermute(other, "hist", cores)
    turned, reached, free = pl.pallas_call(
        ahead_kernel,
        out_shape=(
            jax.ShapeDtypeStruct((block, block * hist_size, 2 * states), F32),
            jax.ShapeDtypeStruct((3, 2, block, 2 * states), F32),
            jax.ShapeDtypeStruct((block, 2 * states), F32),
        ),
        in_specs=[VMEM, VMEM, VMEM, VMEM, VMEM],
        out_specs=(VMEM, VMEM, VMEM),
        compiler_params=grant(8),
        cost_estimate=pl.CostEstimate(flops=4_000_000, bytes_accessed=400_000, transcendentals=1024),
        name="ahead",
    )(
        step,
        jnp.transpose(predicted_row, (0, 2, 1)),
        pseudo_history,
        connection.T,
        state_energy.reshape(1, states),
    )
    paired = pl.pallas_call(
        add_kernel,
        out_shape=tiles,
        in_specs=[VMEM, VMEM, ANY],
        out_specs=VMEM,
        compiler_params=grant(8),
        name="add_pair",
    )(own, swapped, free)
    half = chips // 2
    same_core = [[2 * (h * half + i) + c for i in range(half) for h in range(2)] for c in range(2)]
    arrived = lax.all_to_all(
        paired, "hist", split_axis=0, concat_axis=0, tiled=True, axis_index_groups=same_core
    )
    shares = jax.ShapeDtypeStruct((chips, 2, 3 * lanes), BF16)
    fresh, own, other = pl.pallas_call(
        rows_kernel,
        out_shape=(jax.ShapeDtypeStruct((18, block, lanes), F32), shares, shares),
        in_specs=[VMEM, VMEM, VMEM, VMEM, VMEM, VMEM, VMEM],
        out_specs=(VMEM, VMEM, VMEM),
        compiler_params=grant(8),
        name="rows",
    )(
        step,
        arrived,
        energy,
        jnp.transpose(diagonal_inverse, (1, 2, 0, 3)),
        multiplicity.reshape(1, lanes),
        turned,
        reached,
    )
    swapped = lax.ppermute(other, "hist", cores)
    lattice, written = pl.pallas_call(
        lattice_kernel,
        out_shape=(
            jax.ShapeDtypeStruct((block, 3, 3, 2, lanes), BF16),
            jax.ShapeDtypeStruct((1, lanes), F32),
        ),
        in_specs=[VMEM],
        out_specs=(VMEM, VMEM),
        compiler_params=grant(8),
        cost_estimate=pl.CostEstimate(flops=10_000, bytes_accessed=60_000, transcendentals=0),
        name="lattice",
    )(fresh)
    paired = pl.pallas_call(
        add_shares_kernel,
        out_shape=jax.ShapeDtypeStruct((chips, ka_size, *shares.shape[1:]), BF16),
        in_specs=[VMEM, VMEM, ANY],
        out_specs=VMEM,
        compiler_params=grant(8),
        name="add_shares",
    )(own, swapped, written)
    same_core = [
        [k * hist_size + 2 * t + c for t in spread(chips) for k in range(ka_size)] for c in range(2)
    ]
    got = lax.all_to_all(
        paired.reshape(ka_size * chips, 2, 3 * lanes),
        ("ka", "hist"),
        split_axis=0,
        concat_axis=0,
        tiled=True,
        axis_index_groups=same_core,
    )
    local, pseudo = pl.pallas_call(
        finish_kernel,
        out_shape=(
            jax.ShapeDtypeStruct((3, 3, 2, block), F32),
            jax.ShapeDtypeStruct((2, block, states), F32),
        ),
        in_specs=[VMEM, VMEM],
        out_specs=(VMEM, VMEM),
        compiler_params=grant(8),
        name="finish",
    )(got, free)
    return (
        jnp.transpose(lattice, (0, 3, 1, 2, 4)),
        jnp.transpose(local, (2, 0, 1, 3)),
        jnp.transpose(pseudo, (0, 2, 1)),
    )


def solution(mesh):
    in_specs = (
        P(),
        P("hist", None, "ka"),
        P("hist", None, None, None, "ka"),
        P("hist", None, None, None, None, "ka"),
        P(None, None, None, "ka"),
        P("ka"),
        P(),
        P(),
        P(None, None, "hist"),
        P("hist", None, None, None),
    )
    out_specs = (
        P("hist", None, None, None, "ka"),
        P(None, None, None, "hist"),
        P(None, None, "hist"),
    )
    return jax.shard_map(
        per_device, mesh=mesh, in_specs=in_specs, out_specs=out_specs, check_vma=False
    )
```

```python
import jax
import jax.numpy as jnp
from jax import lax
from jax.experimental import pallas as pl
from jax.experimental.pallas import tpu as pltpu
from jax.sharding import PartitionSpec as P

time_step = 0.05
coupling = 0.02
F32 = jnp.float32
BF16 = jnp.bfloat16
HIGHEST = lax.Precision.HIGHEST
TERMS = 80
CHUNKS = 4


def slot_of(chip, chips):
    half = chips // 2
    return lax.rem(chip, half) * 2 + lax.div(chip, half)


def alternate(order):
    return [h * len(order) + i for i in order for h in range(2)]


def spread(chips):
    half = chips // 2
    bits = half.bit_length() - 1
    order = [sum((i >> b & 1) << (bits - 1 - b) for b in range(bits)) for i in range(half)]
    return alternate(order)


def flag(condition):
    return jnp.where(condition, 1.0, 0.0).astype(F32)


def low_half(lanes=128):
    return lax.broadcasted_iota(jnp.int32, (8, lanes), 0) < 4


def high_low(x):
    high = x.astype(BF16).astype(F32)
    return jnp.where(low_half(x.shape[1]), high, x - high)


def interleave(p, q):
    low = low_half(p.shape[1])
    return jnp.where(low, p, pltpu.roll(q, 4, 0)), jnp.where(low, pltpu.roll(p, 4, 0), q)


def terms_kernel(
    step, kernel_row, energy, history, own, other, current_row, kernel_here, energy_here, coeff, store, few, sems
):
    position = lax.axis_index("hist")
    wide = history.shape[4] // CHUNKS

    def fetch(i):
        columns = pl.ds(pl.multiple_of(i * wide, wide), wide)
        return pltpu.make_async_copy(
            history.at[:, :, :, :, columns, :], store.at[:, :, :, :, columns, :], sems.at[i]
        )

    small = [
        pltpu.make_async_copy(kernel_row, kernel_here, few.at[0]),
        pltpu.make_async_copy(energy, energy_here, few.at[1]),
    ]
    for copy in small:
        copy.start()
    for i in range(CHUNKS):
        fetch(i).start()
    for copy in small:
        copy.wait()
    current = step[0]
    block = energy.shape[1]
    lanes = energy.shape[2]
    current_row[...] = jnp.full((1, lanes), current, jnp.int32)
    zero = jnp.zeros((1, lanes), F32)
    total = jnp.zeros((3, lanes), F32)
    for m in range(block):
        time = position * block + m
        weight = jnp.where(time < current, jnp.where(time == 0, 0.5, 1.0), 0.0).astype(F32)
        total = total + energy_here[:, m, :] * flag(time < current)
        for a in range(3):
            for b in range(3):
                rows = kernel_here[m, a, b].astype(F32) * weight
                re, im = rows[0:1], rows[1:2]
                for i, x in enumerate((re, re + im, im - re)):
                    coeff[m, i, a, b] = jnp.broadcast_to(x, (8, lanes))
    energies = high_low(jnp.concatenate([total, zero, total, zero], axis=0))
    even_core = position % 2 == 0

    def sixteen(start, pair):
        groups = [[], []]
        for c in range(3):
            acc = {}
            for m in range(block):
                for b in range(3):
                    columns = pl.ds(pl.multiple_of(start, 16), 16)
                    re = store[m, 0, b, c, columns, :].astype(F32)
                    im = store[m, 1, b, c, columns, :].astype(F32)
                    both = re + im
                    for a in range(3):
                        weights = [coeff[m, i, a, b] for i in range(3)]
                        for g in range(2):
                            rows = slice(8 * g, 8 * g + 8)
                            for i, x in enumerate((both, im, re)):
                                x = weights[i] * x[rows]
                                acc[i, a, g] = x if m + b == 0 else acc[i, a, g] + x
            for a in range(3):
                for g in range(2):
                    x = acc[0, a, g]
                    acc[0, a, g], acc[1, a, g] = x - acc[1, a, g], x + acc[2, a, g]
            for g in range(2):
                groups[g] += [acc[s, a, g] for s in range(2) for a in range(3)]
        for g in range(2):
            chip = pair + g
            evens, odds = [], []

            def add(p, q):
                x, y = interleave(p, q)
                evens.append(x)
                odds.append(y)

            for u in range(9):
                add(groups[g][2 * u], groups[g][2 * u + 1])
            evens.append(energies * flag(position > 2 * chip))
            odds.append(energies * flag(position > 2 * chip + 1))
            even = jnp.concatenate(evens, axis=0).astype(BF16)
            odd = jnp.concatenate(odds, axis=0).astype(BF16)
            slot = slot_of(chip, own.shape[0])
            own[slot] = jnp.where(even_core, even, odd)
            other[slot] = jnp.where(even_core, odd, even)

    @pl.loop(0, CHUNKS)
    def _(i):
        fetch(i).wait()

        @pl.loop(0, wide // 16)
        def _(h):
            sixteen(i * wide + h * 16, i * (wide // 8) + 2 * h)


def add_kernel(own, arrived, _, out):
    @pl.loop(0, own.shape[0] // 4)
    def _(i):
        for u in range(4):
            t = 4 * i + u
            x = own[t].astype(F32) + arrived[t].astype(F32)
            energies = x[72:80]
            energies = high_low(energies + pltpu.roll(energies, 4, 0))
            out[t] = jnp.concatenate([x[:72], energies], axis=0).astype(BF16)


def signed_swap(x):
    lanes = x.shape[1]
    swapped = pltpu.roll(x, lanes // 2, 1)
    lower = lax.broadcasted_iota(jnp.int32, x.shape, 1) < lanes // 2
    return jnp.where(lower, -swapped, swapped)


def ahead_kernel(step, predicted, pseudo, links, levels, turned, reached, free):
    current, position = step[...], lax.axis_index("hist")
    block, states = predicted.shape[1], predicted.shape[2]
    for m in range(block):
        both = jnp.concatenate([pseudo[m, 0], pseudo[m, 1]], axis=0).astype(F32)
        turned[m] = both.T
    column = lax.broadcasted_iota(jnp.int32, (block, 2 * states), 0) + position * block
    weight = jnp.where(column < current, jnp.where(column == 0, 0.5, 1.0), 0.0) * coupling
    state = lax.broadcasted_iota(jnp.int32, (states, states), 0)
    for a in range(3):
        link = flag(links[2 * a : 2 * a + 1, :] == state) + flag(links[2 * a + 1 : 2 * a + 2, :] == state)
        link = jnp.concatenate([link, link], axis=1)
        for p in range(2):
            x = jnp.concatenate([predicted[p], predicted[p]], axis=0)
            x = jnp.dot(x, link, precision=HIGHEST, preferred_element_type=F32)
            reached[a, p] = x[:block] * weight.astype(F32)
    elapsed = (current - column).astype(F32)
    level = jnp.concatenate([levels[...], levels[...]], axis=1)
    spin = level * time_step * elapsed
    lower = lax.broadcasted_iota(jnp.int32, spin.shape, 1) < states
    free[...] = jnp.where(lower, -jnp.sin(spin), -jnp.cos(spin)) * (column <= current).astype(F32)


def rows_kernel(step, arrived, energy, inverse, multiplicity, turned, reached, fresh, own, other):
    current, position = step[...], lax.axis_index("hist")
    block = energy.shape[1]
    lanes = energy.shape[2]
    got = arrived[0].astype(F32)
    for i in range(1, arrived.shape[0]):
        got = got + arrived[i].astype(F32)
    later = got[72:75] + got[76:79]
    ends = []
    for m in reversed(range(block)):
        later = later + energy[:, m, :] * flag(position * block + m < current)
        ends.append(later)
    angle = jnp.concatenate(
        [ends[block - 1 - j][a : a + 1] for a in range(3) for j in range(block)], axis=0
    )
    angle = angle * time_step
    column = lax.broadcasted_iota(jnp.int32, angle.shape, 0) % block + position * block
    in_range = (column <= current).astype(F32)
    free = [-jnp.sin(angle) * in_range, -jnp.cos(angle) * in_range]

    def right(s, b, c):
        r = ((c * 2 + s) * 3 + b) * block
        x = got[r : r + block]
        return x + free[s][b * block : (b + 1) * block] if b == c else x

    entries = {}
    for c in range(3):
        side = {(s, b): right(s, b, c) for s in range(2) for b in range(3)}
        for a in range(3):
            re = im = 0.0
            for b in range(3):
                dr, di = inverse[a, b, 0:1, :], inverse[a, b, 1:2, :]
                re = re + dr * side[0, b] - di * side[1, b]
                im = im + dr * side[1, b] + di * side[0, b]
            entries[a, c, 0], entries[a, c, 1] = re, im
    entries = [entries[a, c, s] for a in range(3) for c in range(3) for s in range(2)]
    for i, x in enumerate(entries):
        fresh[i] = x
    shared = multiplicity[...].astype(F32)
    even_core = position % 2 == 0
    real = imag = 0.0
    for a in range(3):
        re = jnp.sum(entries[8 * a] * shared, axis=1, keepdims=True)
        im = jnp.sum(entries[8 * a + 1] * shared, axis=1, keepdims=True)
        real = real + re * reached[a, 0] - im * reached[a, 1]
        imag = imag + re * reached[a, 1] + im * reached[a, 0]
    entries += [jnp.ones((1, lanes), F32), jnp.zeros((lanes - 73, lanes), F32)]
    table = jnp.concatenate(entries, axis=0)
    weights = jnp.broadcast_to(shared, (8, lanes))
    message = lax.dot_general(
        weights, table, (((1,), (1,)), ((), ())), precision=HIGHEST, preferred_element_type=F32
    )[0:1]
    high = message.astype(BF16).astype(F32)
    message = jnp.concatenate([high, message - high], axis=0)
    for t in range(own.shape[0]):
        x = y = 0.0
        for m in range(block):
            past = turned[m, 8 * t : 8 * t + 8, :]
            x = x + real[m : m + 1] * past
            y = y + imag[m : m + 1] * past
        x = x + signed_swap(y)
        tile = []
        for core in range(2):
            pairs = [x[4 * core : 4 * core + 2], x[4 * core + 2 : 4 * core + 4]]
            pairs.append(message * flag(position == 2 * t + core))
            tile.append(jnp.concatenate(pairs, axis=1).astype(BF16))
        own[t] = jnp.where(even_core, tile[0], tile[1])
        other[t] = jnp.where(even_core, tile[1], tile[0])


def add_shares_kernel(own, arrived, _, out):
    for i, t in enumerate(spread(own.shape[0])):
        tile = (own[t].astype(F32) + arrived[t].astype(F32)).astype(BF16)
        for k in range(out.shape[1]):
            out[i, k] = tile


def lattice_kernel(fresh, lattice, written):
    written[...] = fresh[0, 0:1]
    for a in range(3):
        for c in range(3):
            i = (a * 3 + c) * 2
            re, im = fresh[i], fresh[i + 1]
            for j in range(lattice.shape[0]):
                pair = jnp.concatenate([re[j : j + 1], im[j : j + 1]], axis=0)
                lattice[j, a, c] = pair.astype(BF16)


def finish_kernel(got, free, local, pseudo):
    parts = []
    for i in range(4):
        x = got[i].astype(F32)
        for k in range(i + 4, got.shape[0], 4):
            x = x + got[k].astype(F32)
        parts.append(x)
    total = (parts[0] + parts[1]) + (parts[2] + parts[3])
    lanes = free.shape[1]
    states = lanes // 2
    sums = total[0:1, 2 * lanes :] + total[1:2, 2 * lanes :]
    count = sums[:, 72:73]
    mean = sums / count
    for a in range(3):
        for c in range(3):
            i = (a * 3 + c) * 8
            local[a, c] = jnp.concatenate([mean[:, i : i + 4], mean[:, i + 4 : i + 8]], axis=0)
    shares = jnp.concatenate([total[:, :lanes], total[:, lanes : 2 * lanes]], axis=0)
    out = free[...] + shares / count
    pseudo[0] = out[:, :states]
    pseudo[1] = out[:, states:]


VMEM = pl.BlockSpec(memory_space=pltpu.VMEM)
HBM = pl.BlockSpec(memory_space=pltpu.HBM)
ANY = pl.BlockSpec(memory_space=pl.ANY)


def grant(mib):
    return pltpu.CompilerParams(vmem_limit_bytes=mib << 20)


def in_hbm(x):
    return pltpu.with_memory_space_constraint(x, pltpu.HBM)


def per_device(
    step_index,
    band_energy,
    kernel_row,
    lattice_history,
    diagonal_inverse,
    multiplicity,
    state_energy,
    connection,
    predicted_row,
    pseudo_history,
):
    block, _, lanes = band_energy.shape
    states, flavours = connection.shape
    ka_size, hist_size = lax.axis_size("ka"), lax.axis_size("hist")
    chips = hist_size // 2
    energy = jnp.transpose(band_energy, (1, 0, 2))
    kernel_pairs = jnp.transpose(kernel_row, (0, 2, 3, 1, 4))
    tiles = jax.ShapeDtypeStruct((chips, TERMS, lanes), BF16)
    cores = [(h, h ^ 1) for h in range(hist_size)]

    own, other, step = pl.pallas_call(
        terms_kernel,
        out_shape=(tiles, tiles, jax.ShapeDtypeStruct((1, lanes), jnp.int32)),
        in_specs=[pl.BlockSpec(memory_space=pltpu.SMEM), HBM, HBM, HBM],
        out_specs=(VMEM, VMEM, VMEM),
        scratch_shapes=[
            pltpu.VMEM(kernel_pairs.shape, BF16),
            pltpu.VMEM(energy.shape, F32),
            pltpu.VMEM((block, 3, 3, 3, 8, lanes), F32),
            pltpu.VMEM(lattice_history.shape, BF16),
            pltpu.SemaphoreType.DMA((2,)),
            pltpu.SemaphoreType.DMA((CHUNKS,)),
        ],
        compiler_params=grant(16),
        name="terms",
    )(step_index, in_hbm(kernel_pairs), in_hbm(energy), in_hbm(lattice_history))
    swapped = lax.ppermute(other, "hist", cores)
    turned, reached, free = pl.pallas_call(
        ahead_kernel,
        out_shape=(
            jax.ShapeDtypeStruct((block, block * hist_size, 2 * states), F32),
            jax.ShapeDtypeStruct((3, 2, block, 2 * states), F32),
            jax.ShapeDtypeStruct((block, 2 * states), F32),
        ),
        in_specs=[VMEM, VMEM, VMEM, VMEM, VMEM],
        out_specs=(VMEM, VMEM, VMEM),
        compiler_params=grant(8),
        cost_estimate=pl.CostEstimate(flops=4_000_000, bytes_accessed=400_000, transcendentals=1024),
        name="ahead",
    )(
        step,
        jnp.transpose(predicted_row, (0, 2, 1)),
        pseudo_history,
        connection.T,
        state_energy.reshape(1, states),
    )
    paired = pl.pallas_call(
        add_kernel,
        out_shape=tiles,
        in_specs=[VMEM, VMEM, ANY],
        out_specs=VMEM,
        compiler_params=grant(8),
        name="add_pair",
    )(own, swapped, free)
    same_core = [[2 * t + c for t in alternate(range(chips // 2))] for c in range(2)]
    arrived = lax.all_to_all(
        paired, "hist", split_axis=0, concat_axis=0, tiled=True, axis_index_groups=same_core
    )
    shares = jax.ShapeDtypeStruct((chips, 2, 3 * lanes), BF16)
    fresh, own, other = pl.pallas_call(
        rows_kernel,
        out_shape=(jax.ShapeDtypeStruct((18, block, lanes), F32), shares, shares),
        in_specs=[VMEM, VMEM, VMEM, VMEM, VMEM, VMEM, VMEM],
        out_specs=(VMEM, VMEM, VMEM),
        compiler_params=grant(8),
        name="rows",
    )(
        step,
        arrived,
        energy,
        jnp.transpose(diagonal_inverse, (1, 2, 0, 3)),
        multiplicity.reshape(1, lanes),
        turned,
        reached,
    )
    swapped = lax.ppermute(other, "hist", cores)
    lattice, written = pl.pallas_call(
        lattice_kernel,
        out_shape=(
            jax.ShapeDtypeStruct((block, 3, 3, 2, lanes), BF16),
            jax.ShapeDtypeStruct((1, lanes), F32),
        ),
        in_specs=[VMEM],
        out_specs=(VMEM, VMEM),
        compiler_params=grant(8),
        cost_estimate=pl.CostEstimate(flops=10_000, bytes_accessed=60_000, transcendentals=0),
        name="lattice",
    )(fresh)
    paired = pl.pallas_call(
        add_shares_kernel,
        out_shape=jax.ShapeDtypeStruct((chips, ka_size, *shares.shape[1:]), BF16),
        in_specs=[VMEM, VMEM, ANY],
        out_specs=VMEM,
        compiler_params=grant(8),
        name="add_shares",
    )(own, swapped, written)
    same_core = [
        [k * hist_size + 2 * t + c for t in spread(chips) for k in alternate(range(ka_size // 2))]
        for c in range(2)
    ]
    got = lax.all_to_all(
        paired.reshape(ka_size * chips, 2, 3 * lanes),
        ("ka", "hist"),
        split_axis=0,
        concat_axis=0,
        tiled=True,
        axis_index_groups=same_core,
    )
    local, pseudo = pl.pallas_call(
        finish_kernel,
        out_shape=(
            jax.ShapeDtypeStruct((3, 3, 2, block), F32),
            jax.ShapeDtypeStruct((2, block, states), F32),
        ),
        in_specs=[VMEM, VMEM],
        out_specs=(VMEM, VMEM),
        compiler_params=grant(8),
        name="finish",
    )(got, free)
    return (
        jnp.transpose(lattice, (0, 3, 1, 2, 4)),
        jnp.transpose(local, (2, 0, 1, 3)),
        jnp.transpose(pseudo, (0, 2, 1)),
    )


def solution(mesh):
    in_specs = (
        P(),
        P("hist", None, "ka"),
        P("hist", None, None, None, "ka"),
        P("hist", None, None, None, None, "ka"),
        P(None, None, None, "ka"),
        P("ka"),
        P(),
        P(),
        P(None, None, "hist"),
        P("hist", None, None, None),
    )
    out_specs = (
        P("hist", None, None, None, "ka"),
        P(None, None, None, "hist"),
        P(None, None, "hist"),
    )
    return jax.shard_map(
        per_device, mesh=mesh, in_specs=in_specs, out_specs=out_specs, check_vma=False
    )
```

```python
import jax
import jax.numpy as jnp
from jax import lax
from jax.experimental import pallas as pl
from jax.experimental.pallas import tpu as pltpu
from jax.sharding import PartitionSpec as P

time_step = 0.05
coupling = 0.02
F32 = jnp.float32
BF16 = jnp.bfloat16
HIGHEST = lax.Precision.HIGHEST
TERMS = 80
CHUNKS = 8


def slot_of(chip, chips):
    half = chips // 2
    return lax.rem(chip, half) * 2 + lax.div(chip, half)


def alternate(order):
    return [h * len(order) + i for i in order for h in range(2)]


def spread(chips):
    half = chips // 2
    bits = half.bit_length() - 1
    order = [sum((i >> b & 1) << (bits - 1 - b) for b in range(bits)) for i in range(half)]
    return alternate(order)


def flag(condition):
    return jnp.where(condition, 1.0, 0.0).astype(F32)


def low_half(lanes=128):
    return lax.broadcasted_iota(jnp.int32, (8, lanes), 0) < 4


def high_low(x):
    high = x.astype(BF16).astype(F32)
    return jnp.where(low_half(x.shape[1]), high, x - high)


def interleave(p, q):
    low = low_half(p.shape[1])
    return jnp.where(low, p, pltpu.roll(q, 4, 0)), jnp.where(low, pltpu.roll(p, 4, 0), q)


def terms_kernel(
    step, kernel_row, energy, history, own, other, current_row, kernel_here, energy_here, coeff, store, few, sems
):
    position = lax.axis_index("hist")
    wide = history.shape[4] // CHUNKS

    def fetch(i):
        columns = pl.ds(pl.multiple_of(i * wide, wide), wide)
        return pltpu.make_async_copy(
            history.at[:, :, :, :, columns, :], store.at[:, :, :, :, columns, :], sems.at[i]
        )

    small = [
        pltpu.make_async_copy(kernel_row, kernel_here, few.at[0]),
        pltpu.make_async_copy(energy, energy_here, few.at[1]),
    ]
    for copy in small:
        copy.start()
    for i in range(4):
        fetch(i).start()
    for copy in small:
        copy.wait()
    current = step[0]
    block = energy.shape[1]
    lanes = energy.shape[2]
    current_row[...] = jnp.full((1, lanes), current, jnp.int32)
    zero = jnp.zeros((1, lanes), F32)
    total = jnp.zeros((3, lanes), F32)
    for m in range(block):
        time = position * block + m
        weight = jnp.where(time < current, jnp.where(time == 0, 0.5, 1.0), 0.0).astype(F32)
        total = total + energy_here[:, m, :] * flag(time < current)
        for a in range(3):
            for b in range(3):
                rows = kernel_here[m, a, b].astype(F32) * weight
                re, im = rows[0:1], rows[1:2]
                for i, x in enumerate((re, re + im, im - re)):
                    coeff[m, i, a, b] = jnp.broadcast_to(x, (8, lanes))
    energies = high_low(jnp.concatenate([total, zero, total, zero], axis=0))
    even_core = position % 2 == 0

    def sixteen(start, pair):
        groups = [[], []]
        for c in range(3):
            acc = {}
            for m in range(block):
                for b in range(3):
                    columns = pl.ds(pl.multiple_of(start, 16), 16)
                    re = store[m, 0, b, c, columns, :].astype(F32)
                    im = store[m, 1, b, c, columns, :].astype(F32)
                    both = re + im
                    for a in range(3):
                        weights = [coeff[m, i, a, b] for i in range(3)]
                        for g in range(2):
                            rows = slice(8 * g, 8 * g + 8)
                            for i, x in enumerate((both, im, re)):
                                x = weights[i] * x[rows]
                                acc[i, a, g] = x if m + b == 0 else acc[i, a, g] + x
            for a in range(3):
                for g in range(2):
                    x = acc[0, a, g]
                    acc[0, a, g], acc[1, a, g] = x - acc[1, a, g], x + acc[2, a, g]
            for g in range(2):
                groups[g] += [acc[s, a, g] for s in range(2) for a in range(3)]
        for g in range(2):
            chip = pair + g
            evens, odds = [], []

            def add(p, q):
                x, y = interleave(p, q)
                evens.append(x)
                odds.append(y)

            for u in range(9):
                add(groups[g][2 * u], groups[g][2 * u + 1])
            evens.append(energies * flag(position > 2 * chip))
            odds.append(energies * flag(position > 2 * chip + 1))
            even = jnp.concatenate(evens, axis=0).astype(BF16)
            odd = jnp.concatenate(odds, axis=0).astype(BF16)
            slot = slot_of(chip, own.shape[0])
            own[slot] = jnp.where(even_core, even, odd)
            other[slot] = jnp.where(even_core, odd, even)

    @pl.loop(0, CHUNKS)
    def _(i):
        fetch(i).wait()

        @pl.when(i + 4 < CHUNKS)
        def _():
            fetch(i + 4).start()

        @pl.loop(0, wide // 16)
        def _(h):
            sixteen(i * wide + h * 16, i * (wide // 8) + 2 * h)


def add_kernel(own, arrived, _, out):
    @pl.loop(0, own.shape[0] // 4)
    def _(i):
        for u in range(4):
            t = 4 * i + u
            x = own[t].astype(F32) + arrived[t].astype(F32)
            energies = x[72:80]
            energies = high_low(energies + pltpu.roll(energies, 4, 0))
            out[t] = jnp.concatenate([x[:72], energies], axis=0).astype(BF16)


def signed_swap(x):
    lanes = x.shape[1]
    swapped = pltpu.roll(x, lanes // 2, 1)
    lower = lax.broadcasted_iota(jnp.int32, x.shape, 1) < lanes // 2
    return jnp.where(lower, -swapped, swapped)


def ahead_kernel(step, predicted, pseudo, links, levels, turned, reached, free):
    current, position = step[...], lax.axis_index("hist")
    block, states = predicted.shape[1], predicted.shape[2]
    for m in range(block):
        both = jnp.concatenate([pseudo[m, 0], pseudo[m, 1]], axis=0).astype(F32)
        turned[m] = both.T
    column = lax.broadcasted_iota(jnp.int32, (block, 2 * states), 0) + position * block
    weight = jnp.where(column < current, jnp.where(column == 0, 0.5, 1.0), 0.0) * coupling
    state = lax.broadcasted_iota(jnp.int32, (states, states), 0)
    for a in range(3):
        link = flag(links[2 * a : 2 * a + 1, :] == state) + flag(links[2 * a + 1 : 2 * a + 2, :] == state)
        link = jnp.concatenate([link, link], axis=1)
        for p in range(2):
            x = jnp.concatenate([predicted[p], predicted[p]], axis=0)
            x = jnp.dot(x, link, precision=HIGHEST, preferred_element_type=F32)
            reached[a, p] = x[:block] * weight.astype(F32)
    elapsed = (current - column).astype(F32)
    level = jnp.concatenate([levels[...], levels[...]], axis=1)
    spin = level * time_step * elapsed
    lower = lax.broadcasted_iota(jnp.int32, spin.shape, 1) < states
    free[...] = jnp.where(lower, -jnp.sin(spin), -jnp.cos(spin)) * (column <= current).astype(F32)


def rows_kernel(step, arrived, energy, inverse, multiplicity, turned, reached, fresh, own, other):
    current, position = step[...], lax.axis_index("hist")
    block = energy.shape[1]
    lanes = energy.shape[2]
    got = arrived[0].astype(F32)
    for i in range(1, arrived.shape[0]):
        got = got + arrived[i].astype(F32)
    later = got[72:75] + got[76:79]
    ends = []
    for m in reversed(range(block)):
        later = later + energy[:, m, :] * flag(position * block + m < current)
        ends.append(later)
    angle = jnp.concatenate(
        [ends[block - 1 - j][a : a + 1] for a in range(3) for j in range(block)], axis=0
    )
    angle = angle * time_step
    column = lax.broadcasted_iota(jnp.int32, angle.shape, 0) % block + position * block
    in_range = (column <= current).astype(F32)
    free = [-jnp.sin(angle) * in_range, -jnp.cos(angle) * in_range]

    def right(s, b, c):
        r = ((c * 2 + s) * 3 + b) * block
        x = got[r : r + block]
        return x + free[s][b * block : (b + 1) * block] if b == c else x

    entries = {}
    for c in range(3):
        side = {(s, b): right(s, b, c) for s in range(2) for b in range(3)}
        for a in range(3):
            re = im = 0.0
            for b in range(3):
                dr, di = inverse[a, b, 0:1, :], inverse[a, b, 1:2, :]
                re = re + dr * side[0, b] - di * side[1, b]
                im = im + dr * side[1, b] + di * side[0, b]
            entries[a, c, 0], entries[a, c, 1] = re, im
    entries = [entries[a, c, s] for a in range(3) for c in range(3) for s in range(2)]
    for i, x in enumerate(entries):
        fresh[i] = x
    shared = multiplicity[...].astype(F32)
    even_core = position % 2 == 0
    real = imag = 0.0
    for a in range(3):
        re = jnp.sum(entries[8 * a] * shared, axis=1, keepdims=True)
        im = jnp.sum(entries[8 * a + 1] * shared, axis=1, keepdims=True)
        real = real + re * reached[a, 0] - im * reached[a, 1]
        imag = imag + re * reached[a, 1] + im * reached[a, 0]
    entries += [jnp.ones((1, lanes), F32), jnp.zeros((lanes - 73, lanes), F32)]
    table = jnp.concatenate(entries, axis=0)
    weights = jnp.broadcast_to(shared, (8, lanes))
    message = lax.dot_general(
        weights, table, (((1,), (1,)), ((), ())), precision=HIGHEST, preferred_element_type=F32
    )[0:1]
    high = message.astype(BF16).astype(F32)
    message = jnp.concatenate([high, message - high], axis=0)
    for t in range(own.shape[0]):
        x = y = 0.0
        for m in range(block):
            past = turned[m, 8 * t : 8 * t + 8, :]
            x = x + real[m : m + 1] * past
            y = y + imag[m : m + 1] * past
        x = x + signed_swap(y)
        tile = []
        for core in range(2):
            pairs = [x[4 * core : 4 * core + 2], x[4 * core + 2 : 4 * core + 4]]
            pairs.append(message * flag(position == 2 * t + core))
            tile.append(jnp.concatenate(pairs, axis=1).astype(BF16))
        own[t] = jnp.where(even_core, tile[0], tile[1])
        other[t] = jnp.where(even_core, tile[1], tile[0])


def add_shares_kernel(own, arrived, _, out):
    for i, t in enumerate(spread(own.shape[0])):
        tile = (own[t].astype(F32) + arrived[t].astype(F32)).astype(BF16)
        for k in range(out.shape[1]):
            out[i, k] = tile


def lattice_kernel(fresh, lattice, written):
    written[...] = fresh[0, 0:1]
    for a in range(3):
        for c in range(3):
            i = (a * 3 + c) * 2
            re, im = fresh[i], fresh[i + 1]
            for j in range(lattice.shape[0]):
                pair = jnp.concatenate([re[j : j + 1], im[j : j + 1]], axis=0)
                lattice[j, a, c] = pair.astype(BF16)


def finish_kernel(got, free, local, pseudo):
    parts = []
    for i in range(4):
        x = got[i].astype(F32)
        for k in range(i + 4, got.shape[0], 4):
            x = x + got[k].astype(F32)
        parts.append(x)
    total = (parts[0] + parts[1]) + (parts[2] + parts[3])
    lanes = free.shape[1]
    states = lanes // 2
    sums = total[0:1, 2 * lanes :] + total[1:2, 2 * lanes :]
    count = sums[:, 72:73]
    mean = sums / count
    pair = jnp.concatenate([mean, pltpu.roll(mean, lanes - 4, 1)], axis=0)
    for a in range(3):
        for c in range(3):
            i = (a * 3 + c) * 8
            local[a, c] = pair[:, i : i + 4]
    shares = jnp.concatenate([total[:, :lanes], total[:, lanes : 2 * lanes]], axis=0)
    out = free[...] + shares / count
    pseudo[0] = out[:, :states]
    pseudo[1] = out[:, states:]


VMEM = pl.BlockSpec(memory_space=pltpu.VMEM)
HBM = pl.BlockSpec(memory_space=pltpu.HBM)
ANY = pl.BlockSpec(memory_space=pl.ANY)


def grant(mib):
    return pltpu.CompilerParams(vmem_limit_bytes=mib << 20)


def in_hbm(x):
    return pltpu.with_memory_space_constraint(x, pltpu.HBM)


def per_device(
    step_index,
    band_energy,
    kernel_row,
    lattice_history,
    diagonal_inverse,
    multiplicity,
    state_energy,
    connection,
    predicted_row,
    pseudo_history,
):
    block, _, lanes = band_energy.shape
    states, flavours = connection.shape
    ka_size, hist_size = lax.axis_size("ka"), lax.axis_size("hist")
    chips = hist_size // 2
    energy = jnp.transpose(band_energy, (1, 0, 2))
    kernel_pairs = jnp.transpose(kernel_row, (0, 2, 3, 1, 4))
    tiles = jax.ShapeDtypeStruct((chips, TERMS, lanes), BF16)
    cores = [(h, h ^ 1) for h in range(hist_size)]

    own, other, step = pl.pallas_call(
        terms_kernel,
        out_shape=(tiles, tiles, jax.ShapeDtypeStruct((1, lanes), jnp.int32)),
        in_specs=[pl.BlockSpec(memory_space=pltpu.SMEM), HBM, HBM, HBM],
        out_specs=(VMEM, VMEM, VMEM),
        scratch_shapes=[
            pltpu.VMEM(kernel_pairs.shape, BF16),
            pltpu.VMEM(energy.shape, F32),
            pltpu.VMEM((block, 3, 3, 3, 8, lanes), F32),
            pltpu.VMEM(lattice_history.shape, BF16),
            pltpu.SemaphoreType.DMA((2,)),
            pltpu.SemaphoreType.DMA((CHUNKS,)),
        ],
        compiler_params=grant(16),
        name="terms",
    )(step_index, in_hbm(kernel_pairs), in_hbm(energy), in_hbm(lattice_history))
    swapped = lax.ppermute(other, "hist", cores)
    turned, reached, free = pl.pallas_call(
        ahead_kernel,
        out_shape=(
            jax.ShapeDtypeStruct((block, block * hist_size, 2 * states), F32),
            jax.ShapeDtypeStruct((3, 2, block, 2 * states), F32),
            jax.ShapeDtypeStruct((block, 2 * states), F32),
        ),
        in_specs=[VMEM, VMEM, VMEM, VMEM, VMEM],
        out_specs=(VMEM, VMEM, VMEM),
        compiler_params=grant(8),
        cost_estimate=pl.CostEstimate(flops=4_000_000, bytes_accessed=400_000, transcendentals=1024),
        name="ahead",
    )(
        step,
        jnp.transpose(predicted_row, (0, 2, 1)),
        pseudo_history,
        connection.T,
        state_energy.reshape(1, states),
    )
    paired = pl.pallas_call(
        add_kernel,
        out_shape=tiles,
        in_specs=[VMEM, VMEM, ANY],
        out_specs=VMEM,
        compiler_params=grant(8),
        name="add_pair",
    )(own, swapped, free)
    same_core = [[2 * t + c for t in alternate(range(chips // 2))] for c in range(2)]
    arrived = lax.all_to_all(
        paired, "hist", split_axis=0, concat_axis=0, tiled=True, axis_index_groups=same_core
    )
    shares = jax.ShapeDtypeStruct((chips, 2, 3 * lanes), BF16)
    fresh, own, other = pl.pallas_call(
        rows_kernel,
        out_shape=(jax.ShapeDtypeStruct((18, block, lanes), F32), shares, shares),
        in_specs=[VMEM, VMEM, VMEM, VMEM, VMEM, VMEM, VMEM],
        out_specs=(VMEM, VMEM, VMEM),
        compiler_params=grant(8),
        name="rows",
    )(
        step,
        arrived,
        energy,
        jnp.transpose(diagonal_inverse, (1, 2, 0, 3)),
        multiplicity.reshape(1, lanes),
        turned,
        reached,
    )
    swapped = lax.ppermute(other, "hist", cores)
    lattice, written = pl.pallas_call(
        lattice_kernel,
        out_shape=(
            jax.ShapeDtypeStruct((block, 3, 3, 2, lanes), BF16),
            jax.ShapeDtypeStruct((1, lanes), F32),
        ),
        in_specs=[VMEM],
        out_specs=(VMEM, VMEM),
        compiler_params=grant(8),
        cost_estimate=pl.CostEstimate(flops=10_000, bytes_accessed=60_000, transcendentals=0),
        name="lattice",
    )(fresh)
    paired = pl.pallas_call(
        add_shares_kernel,
        out_shape=jax.ShapeDtypeStruct((chips, ka_size, *shares.shape[1:]), BF16),
        in_specs=[VMEM, VMEM, ANY],
        out_specs=VMEM,
        compiler_params=grant(8),
        name="add_shares",
    )(own, swapped, written)
    same_core = [
        [k * hist_size + 2 * t + c for t in spread(chips) for k in alternate(range(ka_size // 2))]
        for c in range(2)
    ]
    got = lax.all_to_all(
        paired.reshape(ka_size * chips, 2, 3 * lanes),
        ("ka", "hist"),
        split_axis=0,
        concat_axis=0,
        tiled=True,
        axis_index_groups=same_core,
    )
    local, pseudo = pl.pallas_call(
        finish_kernel,
        out_shape=(
            jax.ShapeDtypeStruct((3, 3, 2, block), F32),
            jax.ShapeDtypeStruct((2, block, states), F32),
        ),
        in_specs=[VMEM, VMEM],
        out_specs=(VMEM, VMEM),
        compiler_params=grant(8),
        name="finish",
    )(got, free)
    return (
        jnp.transpose(lattice, (0, 3, 1, 2, 4)),
        jnp.transpose(local, (2, 0, 1, 3)),
        jnp.transpose(pseudo, (0, 2, 1)),
    )


def solution(mesh):
    in_specs = (
        P(),
        P("hist", None, "ka"),
        P("hist", None, None, None, "ka"),
        P("hist", None, None, None, None, "ka"),
        P(None, None, None, "ka"),
        P("ka"),
        P(),
        P(),
        P(None, None, "hist"),
        P("hist", None, None, None),
    )
    out_specs = (
        P("hist", None, None, None, "ka"),
        P(None, None, None, "hist"),
        P(None, None, "hist"),
    )
    return jax.shard_map(
        per_device, mesh=mesh, in_specs=in_specs, out_specs=out_specs, check_vma=False
    )
```

```python
import jax
import jax.numpy as jnp
from jax import lax
from jax.experimental import pallas as pl
from jax.experimental.pallas import tpu as pltpu
from jax.sharding import PartitionSpec as P

time_step = 0.05
coupling = 0.02
F32 = jnp.float32
BF16 = jnp.bfloat16
HIGHEST = lax.Precision.HIGHEST
TERMS = 80
CHUNKS = 8


def slot_of(chip, chips):
    return lax.rem(lax.rem(chip, 8) * 5, 8) * 2 + lax.div(chip, 8)


def alternate(order):
    return [h * len(order) + i for i in order for h in range(2)]


def spread(chips):
    half = chips // 2
    bits = half.bit_length() - 1
    order = [sum((i >> b & 1) << (bits - 1 - b) for b in range(bits)) for i in range(half)]
    return alternate(order)


def flag(condition):
    return jnp.where(condition, 1.0, 0.0).astype(F32)


def low_half(lanes=128):
    return lax.broadcasted_iota(jnp.int32, (8, lanes), 0) < 4


def high_low(x):
    high = x.astype(BF16).astype(F32)
    return jnp.where(low_half(x.shape[1]), high, x - high)


def interleave(p, q):
    low = low_half(p.shape[1])
    return jnp.where(low, p, pltpu.roll(q, 4, 0)), jnp.where(low, pltpu.roll(p, 4, 0), q)


def terms_kernel(
    step, kernel_row, energy, history, own, other, current_row, kernel_here, energy_here, coeff, store, few, sems
):
    position = lax.axis_index("hist")
    wide = history.shape[4] // CHUNKS

    def fetch(i):
        columns = pl.ds(pl.multiple_of(i * wide, wide), wide)
        return pltpu.make_async_copy(
            history.at[:, :, :, :, columns, :], store.at[:, :, :, :, columns, :], sems.at[i]
        )

    small = [
        pltpu.make_async_copy(kernel_row, kernel_here, few.at[0]),
        pltpu.make_async_copy(energy, energy_here, few.at[1]),
    ]
    for copy in small:
        copy.start()
    for i in range(4):
        fetch(i).start()
    for copy in small:
        copy.wait()
    current = step[0]
    block = energy.shape[1]
    lanes = energy.shape[2]
    current_row[...] = jnp.full((1, lanes), current, jnp.int32)
    zero = jnp.zeros((1, lanes), F32)
    total = jnp.zeros((3, lanes), F32)
    for m in range(block):
        time = position * block + m
        weight = jnp.where(time < current, jnp.where(time == 0, 0.5, 1.0), 0.0).astype(F32)
        total = total + energy_here[:, m, :] * flag(time < current)
        for a in range(3):
            for b in range(3):
                rows = kernel_here[m, a, b].astype(F32) * weight
                re, im = rows[0:1], rows[1:2]
                for i, x in enumerate((re, re + im, im - re)):
                    coeff[m, i, a, b] = jnp.broadcast_to(x, (8, lanes))
    energies = high_low(jnp.concatenate([total, zero, total, zero], axis=0))
    even_core = position % 2 == 0

    def sixteen(start, pair):
        groups = [[], []]
        for c in range(3):
            acc = {}
            for m in range(block):
                for b in range(3):
                    columns = pl.ds(pl.multiple_of(start, 16), 16)
                    re = store[m, 0, b, c, columns, :].astype(F32)
                    im = store[m, 1, b, c, columns, :].astype(F32)
                    both = re + im
                    for a in range(3):
                        weights = [coeff[m, i, a, b] for i in range(3)]
                        for g in range(2):
                            rows = slice(8 * g, 8 * g + 8)
                            for i, x in enumerate((both, im, re)):
                                x = weights[i] * x[rows]
                                acc[i, a, g] = x if m + b == 0 else acc[i, a, g] + x
            for a in range(3):
                for g in range(2):
                    x = acc[0, a, g]
                    acc[0, a, g], acc[1, a, g] = x - acc[1, a, g], x + acc[2, a, g]
            for g in range(2):
                groups[g] += [acc[s, a, g] for s in range(2) for a in range(3)]
        for g in range(2):
            chip = pair + g
            evens, odds = [], []

            def add(p, q):
                x, y = interleave(p, q)
                evens.append(x)
                odds.append(y)

            for u in range(9):
                add(groups[g][2 * u], groups[g][2 * u + 1])
            evens.append(energies * flag(position > 2 * chip))
            odds.append(energies * flag(position > 2 * chip + 1))
            even = jnp.concatenate(evens, axis=0).astype(BF16)
            odd = jnp.concatenate(odds, axis=0).astype(BF16)
            slot = slot_of(chip, own.shape[0])
            own[slot] = jnp.where(even_core, even, odd)
            other[slot] = jnp.where(even_core, odd, even)

    @pl.loop(0, CHUNKS)
    def _(i):
        fetch(i).wait()

        @pl.when(i + 4 < CHUNKS)
        def _():
            fetch(i + 4).start()

        @pl.loop(0, wide // 16)
        def _(h):
            sixteen(i * wide + h * 16, i * (wide // 8) + 2 * h)


def add_kernel(own, arrived, _, out):
    @pl.loop(0, own.shape[0] // 4)
    def _(i):
        for u in range(4):
            t = 4 * i + u
            x = own[t].astype(F32) + arrived[t].astype(F32)
            energies = x[72:80]
            energies = high_low(energies + pltpu.roll(energies, 4, 0))
            out[t] = jnp.concatenate([x[:72], energies], axis=0).astype(BF16)


def signed_swap(x):
    lanes = x.shape[1]
    swapped = pltpu.roll(x, lanes // 2, 1)
    lower = lax.broadcasted_iota(jnp.int32, x.shape, 1) < lanes // 2
    return jnp.where(lower, -swapped, swapped)


def ahead_kernel(step, predicted, pseudo, links, levels, turned, reached, free):
    current, position = step[...], lax.axis_index("hist")
    block, states = predicted.shape[1], predicted.shape[2]
    for m in range(block):
        both = jnp.concatenate([pseudo[m, 0], pseudo[m, 1]], axis=0).astype(F32)
        turned[m] = both.T
    column = lax.broadcasted_iota(jnp.int32, (block, 2 * states), 0) + position * block
    weight = jnp.where(column < current, jnp.where(column == 0, 0.5, 1.0), 0.0) * coupling
    state = lax.broadcasted_iota(jnp.int32, (states, states), 0)
    for a in range(3):
        link = flag(links[2 * a : 2 * a + 1, :] == state) + flag(links[2 * a + 1 : 2 * a + 2, :] == state)
        link = jnp.concatenate([link, link], axis=1)
        for p in range(2):
            x = jnp.concatenate([predicted[p], predicted[p]], axis=0)
            x = jnp.dot(x, link, precision=HIGHEST, preferred_element_type=F32)
            reached[a, p] = x[:block] * weight.astype(F32)
    elapsed = (current - column).astype(F32)
    level = jnp.concatenate([levels[...], levels[...]], axis=1)
    spin = level * time_step * elapsed
    lower = lax.broadcasted_iota(jnp.int32, spin.shape, 1) < states
    free[...] = jnp.where(lower, -jnp.sin(spin), -jnp.cos(spin)) * (column <= current).astype(F32)


def rows_kernel(step, arrived, energy, inverse, multiplicity, turned, reached, fresh, own, other):
    current, position = step[...], lax.axis_index("hist")
    block = energy.shape[1]
    lanes = energy.shape[2]
    got = arrived[0].astype(F32)
    for i in range(1, arrived.shape[0]):
        got = got + arrived[i].astype(F32)
    later = got[72:75] + got[76:79]
    ends = []
    for m in reversed(range(block)):
        later = later + energy[:, m, :] * flag(position * block + m < current)
        ends.append(later)
    angle = jnp.concatenate(
        [ends[block - 1 - j][a : a + 1] for a in range(3) for j in range(block)], axis=0
    )
    angle = angle * time_step
    column = lax.broadcasted_iota(jnp.int32, angle.shape, 0) % block + position * block
    in_range = (column <= current).astype(F32)
    free = [-jnp.sin(angle) * in_range, -jnp.cos(angle) * in_range]

    def right(s, b, c):
        r = ((c * 2 + s) * 3 + b) * block
        x = got[r : r + block]
        return x + free[s][b * block : (b + 1) * block] if b == c else x

    entries = {}
    for c in range(3):
        side = {(s, b): right(s, b, c) for s in range(2) for b in range(3)}
        for a in range(3):
            re = im = 0.0
            for b in range(3):
                dr, di = inverse[a, b, 0:1, :], inverse[a, b, 1:2, :]
                re = re + dr * side[0, b] - di * side[1, b]
                im = im + dr * side[1, b] + di * side[0, b]
            entries[a, c, 0], entries[a, c, 1] = re, im
    entries = [entries[a, c, s] for a in range(3) for c in range(3) for s in range(2)]
    for i, x in enumerate(entries):
        fresh[i] = x
    shared = multiplicity[...].astype(F32)
    even_core = position % 2 == 0
    real = imag = 0.0
    for a in range(3):
        re = jnp.sum(entries[8 * a] * shared, axis=1, keepdims=True)
        im = jnp.sum(entries[8 * a + 1] * shared, axis=1, keepdims=True)
        real = real + re * reached[a, 0] - im * reached[a, 1]
        imag = imag + re * reached[a, 1] + im * reached[a, 0]
    entries += [jnp.ones((1, lanes), F32), jnp.zeros((lanes - 73, lanes), F32)]
    table = jnp.concatenate(entries, axis=0)
    weights = jnp.broadcast_to(shared, (8, lanes))
    message = lax.dot_general(
        weights, table, (((1,), (1,)), ((), ())), precision=HIGHEST, preferred_element_type=F32
    )[0:1]
    high = message.astype(BF16).astype(F32)
    message = jnp.concatenate([high, message - high], axis=0)
    for t in range(own.shape[0]):
        x = y = 0.0
        for m in range(block):
            past = turned[m, 8 * t : 8 * t + 8, :]
            x = x + real[m : m + 1] * past
            y = y + imag[m : m + 1] * past
        x = x + signed_swap(y)
        tile = []
        for core in range(2):
            pairs = [x[4 * core : 4 * core + 2], x[4 * core + 2 : 4 * core + 4]]
            pairs.append(message * flag(position == 2 * t + core))
            tile.append(jnp.concatenate(pairs, axis=1).astype(BF16))
        own[t] = jnp.where(even_core, tile[0], tile[1])
        other[t] = jnp.where(even_core, tile[1], tile[0])


def add_shares_kernel(own, arrived, _, out):
    for i, t in enumerate(spread(own.shape[0])):
        tile = (own[t].astype(F32) + arrived[t].astype(F32)).astype(BF16)
        for k in range(out.shape[1]):
            out[i, k] = tile


def lattice_kernel(fresh, lattice, written):
    written[...] = fresh[0, 0:1]
    for a in range(3):
        for c in range(3):
            i = (a * 3 + c) * 2
            re, im = fresh[i], fresh[i + 1]
            for j in range(lattice.shape[0]):
                pair = jnp.concatenate([re[j : j + 1], im[j : j + 1]], axis=0)
                lattice[j, a, c] = pair.astype(BF16)


def finish_kernel(got, free, local, pseudo):
    parts = []
    for i in range(4):
        x = got[i].astype(F32)
        for k in range(i + 4, got.shape[0], 4):
            x = x + got[k].astype(F32)
        parts.append(x)
    total = (parts[0] + parts[1]) + (parts[2] + parts[3])
    lanes = free.shape[1]
    states = lanes // 2
    sums = total[0:1, 2 * lanes :] + total[1:2, 2 * lanes :]
    count = sums[:, 72:73]
    mean = sums / count
    pair = jnp.concatenate([mean, pltpu.roll(mean, lanes - 4, 1)], axis=0)
    for a in range(3):
        for c in range(3):
            i = (a * 3 + c) * 8
            local[a, c] = pair[:, i : i + 4]
    shares = jnp.concatenate([total[:, :lanes], total[:, lanes : 2 * lanes]], axis=0)
    out = free[...] + shares / count
    pseudo[0] = out[:, :states]
    pseudo[1] = out[:, states:]


VMEM = pl.BlockSpec(memory_space=pltpu.VMEM)
HBM = pl.BlockSpec(memory_space=pltpu.HBM)
ANY = pl.BlockSpec(memory_space=pl.ANY)


def grant(mib):
    return pltpu.CompilerParams(vmem_limit_bytes=mib << 20)


def in_hbm(x):
    return pltpu.with_memory_space_constraint(x, pltpu.HBM)


def per_device(
    step_index,
    band_energy,
    kernel_row,
    lattice_history,
    diagonal_inverse,
    multiplicity,
    state_energy,
    connection,
    predicted_row,
    pseudo_history,
):
    block, _, lanes = band_energy.shape
    states, flavours = connection.shape
    ka_size, hist_size = lax.axis_size("ka"), lax.axis_size("hist")
    chips = hist_size // 2
    energy = jnp.transpose(band_energy, (1, 0, 2))
    kernel_pairs = jnp.transpose(kernel_row, (0, 2, 3, 1, 4))
    tiles = jax.ShapeDtypeStruct((chips, TERMS, lanes), BF16)
    cores = [(h, h ^ 1) for h in range(hist_size)]

    own, other, step = pl.pallas_call(
        terms_kernel,
        out_shape=(tiles, tiles, jax.ShapeDtypeStruct((1, lanes), jnp.int32)),
        in_specs=[pl.BlockSpec(memory_space=pltpu.SMEM), HBM, HBM, HBM],
        out_specs=(VMEM, VMEM, VMEM),
        scratch_shapes=[
            pltpu.VMEM(kernel_pairs.shape, BF16),
            pltpu.VMEM(energy.shape, F32),
            pltpu.VMEM((block, 3, 3, 3, 8, lanes), F32),
            pltpu.VMEM(lattice_history.shape, BF16),
            pltpu.SemaphoreType.DMA((2,)),
            pltpu.SemaphoreType.DMA((CHUNKS,)),
        ],
        compiler_params=grant(16),
        name="terms",
    )(step_index, in_hbm(kernel_pairs), in_hbm(energy), in_hbm(lattice_history))
    swapped = lax.ppermute(other, "hist", cores)
    turned, reached, free = pl.pallas_call(
        ahead_kernel,
        out_shape=(
            jax.ShapeDtypeStruct((block, block * hist_size, 2 * states), F32),
            jax.ShapeDtypeStruct((3, 2, block, 2 * states), F32),
            jax.ShapeDtypeStruct((block, 2 * states), F32),
        ),
        in_specs=[VMEM, VMEM, VMEM, VMEM, VMEM],
        out_specs=(VMEM, VMEM, VMEM),
        compiler_params=grant(8),
        cost_estimate=pl.CostEstimate(flops=4_000_000, bytes_accessed=400_000, transcendentals=1024),
        name="ahead",
    )(
        step,
        jnp.transpose(predicted_row, (0, 2, 1)),
        pseudo_history,
        connection.T,
        state_energy.reshape(1, states),
    )
    paired = pl.pallas_call(
        add_kernel,
        out_shape=tiles,
        in_specs=[VMEM, VMEM, ANY],
        out_specs=VMEM,
        compiler_params=grant(8),
        name="add_pair",
    )(own, swapped, free)
    same_core = [[2 * t + c for t in alternate([5 * i % 8 for i in range(8)])] for c in range(2)]
    arrived = lax.all_to_all(
        paired, "hist", split_axis=0, concat_axis=0, tiled=True, axis_index_groups=same_core
    )
    shares = jax.ShapeDtypeStruct((chips, 2, 3 * lanes), BF16)
    fresh, own, other = pl.pallas_call(
        rows_kernel,
        out_shape=(jax.ShapeDtypeStruct((18, block, lanes), F32), shares, shares),
        in_specs=[VMEM, VMEM, VMEM, VMEM, VMEM, VMEM, VMEM],
        out_specs=(VMEM, VMEM, VMEM),
        compiler_params=grant(8),
        name="rows",
    )(
        step,
        arrived,
        energy,
        jnp.transpose(diagonal_inverse, (1, 2, 0, 3)),
        multiplicity.reshape(1, lanes),
        turned,
        reached,
    )
    swapped = lax.ppermute(other, "hist", cores)
    lattice, written = pl.pallas_call(
        lattice_kernel,
        out_shape=(
            jax.ShapeDtypeStruct((block, 3, 3, 2, lanes), BF16),
            jax.ShapeDtypeStruct((1, lanes), F32),
        ),
        in_specs=[VMEM],
        out_specs=(VMEM, VMEM),
        compiler_params=grant(8),
        cost_estimate=pl.CostEstimate(flops=10_000, bytes_accessed=60_000, transcendentals=0),
        name="lattice",
    )(fresh)
    paired = pl.pallas_call(
        add_shares_kernel,
        out_shape=jax.ShapeDtypeStruct((chips, ka_size, *shares.shape[1:]), BF16),
        in_specs=[VMEM, VMEM, ANY],
        out_specs=VMEM,
        compiler_params=grant(8),
        name="add_shares",
    )(own, swapped, written)
    same_core = [
        [k * hist_size + 2 * t + c for t in spread(chips) for k in alternate(range(ka_size // 2))]
        for c in range(2)
    ]
    got = lax.all_to_all(
        paired.reshape(ka_size * chips, 2, 3 * lanes),
        ("ka", "hist"),
        split_axis=0,
        concat_axis=0,
        tiled=True,
        axis_index_groups=same_core,
    )
    local, pseudo = pl.pallas_call(
        finish_kernel,
        out_shape=(
            jax.ShapeDtypeStruct((3, 3, 2, block), F32),
            jax.ShapeDtypeStruct((2, block, states), F32),
        ),
        in_specs=[VMEM, VMEM],
        out_specs=(VMEM, VMEM),
        compiler_params=grant(8),
        name="finish",
    )(got, free)
    return (
        jnp.transpose(lattice, (0, 3, 1, 2, 4)),
        jnp.transpose(local, (2, 0, 1, 3)),
        jnp.transpose(pseudo, (0, 2, 1)),
    )


def solution(mesh):
    in_specs = (
        P(),
        P("hist", None, "ka"),
        P("hist", None, None, None, "ka"),
        P("hist", None, None, None, None, "ka"),
        P(None, None, None, "ka"),
        P("ka"),
        P(),
        P(),
        P(None, None, "hist"),
        P("hist", None, None, None),
    )
    out_specs = (
        P("hist", None, None, None, "ka"),
        P(None, None, None, "hist"),
        P(None, None, "hist"),
    )
    return jax.shard_map(
        per_device, mesh=mesh, in_specs=in_specs, out_specs=out_specs, check_vma=False
    )
```
